512 devices in a mesh: slab: 16 (over z_lo, core), src: 32 (over y, x, z_hi).
Axes of the slice: x: 4, y: 4, z: 16 (z_hi: 2, z_lo: 8; z = z_hi * 8 + z_lo), core: 2. Of those that a mesh axis runs over, the one named last changes fastest.
Arguments:
- trace_values: bfloat16 [32, 8192, 128], P('src', 'slab'), may hold values from -6 to 6
- trace_owner: int32 [32, 8192, 1], P('src', 'slab'), may hold values from 0 to 15; in each aligned block of 512 rows (0 to 511, 512 to 1023, ..., all dimensions but the last counted through in order) at most 64 rows name the same one
- trace_source: int32 [32, 8192], P('src', 'slab'), may hold values from 0 to 511
- source_fields: bfloat16 [2, 8192, 16384], P(None, 'slab', 'src'), may hold values from -0.03125 to 0.03125
- green_fields: bfloat16 [2, 2048, 16384], P(None, 'slab', 'src'), may hold values from -0.0625 to 0.0625
Outputs:
- gradient: float32 [16384], P('src')
The draws below stay inside these ranges and needn't reach their ends.
Inputs may be any that keep to these rules, and one draw needn't show every extreme that they name: `trace_owner`: among the traces of one device, no owner is named by more than 64 traces, a bound that some block reaches.
All inputs are finite; a program needn't handle non-finite values.
Results may differ from the reference program's by a relative error of at most 0.0026.
Values may be sent and summed in bfloat16 or wider, within the bound.
A program may use at most 64 MiB of HBM per device.

```python
import math
import jax
import jax.numpy as jnp
import numpy as np
from jax import lax

NREC = 2048
S_DEV = 512
M_DEV = 512
TR_DEV = 512
CAP = 64
NSRC = 8192
M = 16384
RB = 64
TRACES = 8192
N_SLAB = 16
N_SRC = 32


def set_ends(values, rng, low, largest):
    longest = values.shape.index(max(values.shape))
    spots = []
    for shift in (0, 1):
        where = [jax.random.randint(jax.random.fold_in(rng, axis), (), 0, length) for axis, length in enumerate(values.shape)]
        where[longest] = (where[longest] + shift) % values.shape[longest]
        spots.append(tuple(where))
    return values.at[spots[0]].set(low).at[spots[1]].set(largest)


def block_scale(stream_key, extent, pieces, low, largest):
    factor_of = 1.0
    for position, blocks in pieces:
        steps = jax.random.uniform(jax.random.fold_in(jax.random.fold_in(stream_key, 6), position), (blocks,), jnp.float32, low / len(pieces), largest / len(pieces))
        factor_of = factor_of * jnp.repeat(jnp.exp(steps), extent[position] // blocks).reshape((-1,) + (1,) * (len(extent) - 1 - position))
    return factor_of


def assign_block(key, own, number, rows, amount, top, most, skew):
    sequence = jax.random.permutation(key, amount)
    packed, usual = portions_of(amount, rows * top, most, skew, True), portions_of(amount, rows * top, most, skew, False)
    places = jnp.arange(amount)

    def named(lengths, offset_by):
        used = int((lengths > 0).sum())
        fixed = max(1, used // 4)
        shifted = fixed + (places - fixed + offset_by * (used - fixed)) % max(1, amount - fixed)
        return jnp.zeros((amount,), jnp.int32).at[sequence[jnp.where(places < fixed, places, shifted)]].set(jnp.asarray(lengths, jnp.int32))

    lengths = jnp.where(number % 4 == 0, named(packed, number // 4), named(usual, number - number // 4 - 1))
    mixed = jax.random.permutation(jax.random.fold_in(own, 3), amount)
    giver, sink = mixed[0:amount // 2 * 2:2], mixed[1:amount // 2 * 2:2]
    slack = jnp.minimum(lengths[giver] - 1, most - lengths[sink]) // 2
    slack = jnp.where((giver == sequence[0]) | (sink == sequence[0]) | (lengths[sink] == 0), 0, jnp.maximum(slack, 0))
    shifted = jax.random.randint(jax.random.fold_in(own, 4), (amount // 2,), 0, 1 << 20) % (slack + 1)
    lengths = lengths.at[giver].add(-shifted).at[sink].add(shifted)
    members = jnp.searchsorted(jnp.cumsum(lengths), jnp.arange(rows * top), side="right").astype(jnp.int32)
    grid = members.reshape(top, rows).T
    grid = grid[jax.random.permutation(jax.random.fold_in(own, 1), rows)]
    offset_by = jax.random.randint(jax.random.fold_in(own, 2), (rows, 1), 0, top)
    return jnp.take_along_axis(grid, (jnp.arange(top)[None, :] + offset_by) % top, axis=1)


def portions_of(count, total, reach, skew, full):
    loads = [(1 << 20) // math.isqrt(rank ** skew) + 1 for rank in range(1, count + 1)]
    largest = reach if full else min(reach, max(-(-total // count), total * loads[0] // sum(loads)))
    least = 1 if total - largest >= count - 1 else 0
    holding, spare = [largest] + [least] * (count - 1), total - largest - least * (count - 1)
    while spare > 0:
        free = [i for i in range(1, count) if holding[i] < largest] or [i for i in range(1, count) if holding[i] < reach]
        pool, left = sum([loads[i] for i in free]), spare
        for i in free:
            extra = min(reach - holding[i], max(1, left * loads[i] // pool), spare)
            holding[i] = holding[i] + extra
            spare = spare - extra
    return np.array(holding)


def bell_draw(key, dims, scale, limit, shards=(), kind=jnp.bfloat16):
    values = jax.random.normal(key, dims, jnp.float32) * scale
    if len(shards) > 0:
        values = block_scale(key, dims, shards, -0.22, 0.18) * values
    return jnp.clip(values, min=-limit, max=limit).astype(kind)


def setup_inputs(seed: int = 0) -> dict:
    arg_keys = jax.random.split(jax.random.key(seed), 6)
    trace_values = bell_draw(arg_keys[0], (N_SRC, TRACES, 2 * RB), 1.0, 6.0, ((0, 32), (1, 16)))
    trace_owner_keys = jax.random.split(jax.random.fold_in(arg_keys[1], 1), N_SRC * TRACES // TR_DEV)
    trace_owner_turns = jax.random.permutation(jax.random.fold_in(arg_keys[1], 3), N_SRC * TRACES // TR_DEV)
    trace_owner = jax.vmap(lambda own, number: assign_block(jax.random.fold_in(arg_keys[1], 2), own, number, TR_DEV, N_SLAB, 1, CAP, 2))(trace_owner_keys, trace_owner_turns).reshape((N_SRC, TRACES, 1))
    trace_source = set_ends(jax.random.randint(arg_keys[2], (N_SRC, TRACES), 0, S_DEV), jax.random.fold_in(arg_keys[2], 1), 0, S_DEV - 1).astype(jnp.int32)
    source_fields = bell_draw(arg_keys[3], (2, NSRC, M), (4 * NSRC) ** -0.5, 0.03125, ((1, 16), (2, 32)))
    green_fields = bell_draw(arg_keys[4], (2, NREC, M), (4 * NREC) ** -0.5, 0.0625, ((1, 16), (2, 32)))
    return dict(trace_values=trace_values, trace_owner=trace_owner, trace_source=trace_source, source_fields=source_fields, green_fields=green_fields)


def reference(trace_values, trace_owner, trace_source, source_fields, green_fields):
    source = trace_owner[:, :, 0] * S_DEV + trace_source

    def assemble(pair):
        ids, values = pair
        summed = jax.ops.segment_sum(values.astype(jnp.float32), ids, num_segments=NSRC)
        return summed.astype(jnp.bfloat16)

    blocks = lax.map(assemble, (source, trace_values))
    blocks = blocks.reshape(N_SRC, NSRC, 2, RB)
    res_re = jnp.transpose(blocks[:, :, 0, :], (1, 0, 2)).reshape(NSRC, NREC)
    res_im = jnp.transpose(blocks[:, :, 1, :], (1, 0, 2)).reshape(NSRC, NREC)

    def image_block(index):
        offset = (index * M_DEV).astype(jnp.int32)
        green_re = lax.dynamic_slice_in_dim(green_fields[0], offset, M_DEV, 1)
        green_im = lax.dynamic_slice_in_dim(green_fields[1], offset, M_DEV, 1)
        field_re = lax.dynamic_slice_in_dim(source_fields[0], offset, M_DEV, 1)
        field_im = lax.dynamic_slice_in_dim(source_fields[1], offset, M_DEV, 1)
        adj_re = jnp.dot(res_re, green_re, preferred_element_type=jnp.float32) + jnp.dot(res_im, green_im, preferred_element_type=jnp.float32)
        adj_im = jnp.dot(res_re, green_im, preferred_element_type=jnp.float32) - jnp.dot(res_im, green_re, preferred_element_type=jnp.float32)
        return jnp.sum(field_re.astype(jnp.float32) * adj_re - field_im.astype(jnp.float32) * adj_im, axis=0)

    gradient = lax.map(image_block, jnp.arange(N_SRC, dtype=jnp.int32))
    return gradient.reshape(M)
```

```python
import jax
import jax.numpy as jnp
from jax import lax
from jax.experimental import pallas as pl
from jax.experimental.pallas import tpu as pltpu
from jax.sharding import PartitionSpec as P

MESH = pl.DeviceIdType.MESH
SLABS = 16
SRCS = 32
CAP = 64
ROWS = 512
CELLS = 512
CHIPS = 8


def kernel(
    owner_ref,
    label_ref,
    values_ref,
    fields_hbm,
    green_hbm,
    out_ref,
    sent,
    sent_labels,
    got,
    got_labels,
    res,
    green,
    fields,
    acc_re,
    acc_im,
    parts,
    load_sem,
    trace_send,
    trace_recv,
    label_send,
    label_recv,
    green_send,
    green_recv,
    pair_send,
    pair_recv,
    res_send,
    res_recv,
    sum_send,
    sum_recv,
):
    slab = lax.axis_index("slab")
    src = lax.axis_index("src")
    z, core = slab // 2, slab % 2
    y, x, h = src // 8, (src // 2) % 4, src % 2

    def at(dx, dy, hh):
        return (((y + dy + 4) % 4) * 4 + (x + dx + 4) % 4) * 2 + hh

    neighbours = (at(1, 0, h), at(-1, 0, h), at(0, 1, h), at(0, -1, h))
    twin = at(0, 0, 1 - h)

    load_green = pltpu.make_async_copy(green_hbm, green.at[slab], load_sem.at[0])
    load_green.start()
    load_fields = pltpu.make_async_copy(fields_hbm, fields, load_sem.at[1])
    load_fields.start()

    barrier = pltpu.get_barrier_semaphore()
    for d in range(1, SLABS):
        pl.semaphore_signal(
            barrier, inc=1, device_id={"slab": (slab + d) % SLABS}, device_id_type=MESH
        )
    for other in neighbours + (twin,):
        pl.semaphore_signal(barrier, inc=1, device_id={"src": other}, device_id_type=MESH)

    owners = owner_ref[...]
    labels = label_ref[...]
    owner_ids = lax.broadcasted_iota(jnp.int32, (SLABS, ROWS), 0)
    hits = owner_ids == owners
    hits_f = hits.astype(jnp.float32)
    earlier = (
        lax.broadcasted_iota(jnp.int32, (ROWS, ROWS), 0)
        < lax.broadcasted_iota(jnp.int32, (ROWS, ROWS), 1)
    )
    counts = jnp.dot(
        hits_f.astype(jnp.bfloat16),
        earlier.astype(jnp.float32).astype(jnp.bfloat16),
        preferred_element_type=jnp.float32,
    )
    ranks = jnp.sum(counts * hits_f, axis=0, keepdims=True).astype(jnp.int32)
    slots = owners * CAP + ranks
    placing = (
        (lax.broadcasted_iota(jnp.int32, (SLABS * CAP, ROWS), 0) == slots)
        .astype(jnp.float32)
        .astype(jnp.bfloat16)
    )
    placed = jnp.dot(placing, values_ref[...], preferred_element_type=jnp.float32)
    sent[...] = placed.astype(jnp.bfloat16).reshape(SLABS, CAP, 128)
    rank_hits = (
        (lax.broadcasted_iota(jnp.int32, (128, ROWS), 0) % CAP == ranks)
        .astype(jnp.float32)
        .astype(jnp.bfloat16)
    )
    high = (labels // 32).astype(jnp.float32)
    low = (labels % 32 + 1).astype(jnp.float32)
    codes = jnp.concatenate([hits_f * high, hits_f * low], axis=0).astype(jnp.bfloat16)
    placed_codes = lax.dot_general(
        codes, rank_hits, (((1,), (1,)), ((), ())), preferred_element_type=jnp.float32
    )
    label_rows = placed_codes[:SLABS] * 32.0 + placed_codes[SLABS:] - 1.0
    for k in range(SLABS):
        sent_labels[k] = label_rows[k : k + 1, :]

    load_green.wait()
    pl.semaphore_wait(barrier, SLABS - 1 + 5)

    def trace_copy(d):
        to = (slab + d) % SLABS
        return (
            pltpu.make_async_remote_copy(
                src_ref=sent.at[to],
                dst_ref=got.at[slab],
                send_sem=trace_send.at[d],
                recv_sem=trace_recv.at[slab],
                device_id={"slab": to},
                device_id_type=MESH,
            ),
            pltpu.make_async_remote_copy(
                src_ref=sent_labels.at[to],
                dst_ref=got_labels.at[slab],
                send_sem=label_send.at[d],
                recv_sem=label_recv.at[slab],
                device_id={"slab": to},
                device_id_type=MESH,
            ),
        )

    def trace_wait(d):
        frm = (slab + d) % SLABS
        pltpu.make_async_copy(got.at[frm], got.at[frm], trace_recv.at[frm]).wait()
        pltpu.make_async_copy(got_labels.at[frm], got_labels.at[frm], label_recv.at[frm]).wait()

    for d in range(1, SLABS):
        for copy in trace_copy(d):
            copy.start()

    def green_copy(step, block, part, way):
        index = block * 2 + core
        to = (slab + 2, slab - 2)[way]
        return pltpu.make_async_remote_copy(
            src_ref=green.at[index, part],
            dst_ref=green.at[index, part],
            send_sem=green_send.at[way, step, part],
            recv_sem=green_recv.at[index, part],
            device_id={"slab": to},
            device_id_type=MESH,
        )

    def pair_copy(block, part):
        index = block * 2 + core
        return pltpu.make_async_remote_copy(
            src_ref=green.at[index, part],
            dst_ref=green.at[index, part],
            send_sem=pair_send.at[block, part],
            recv_sem=pair_recv.at[block, part],
            device_id={"slab": z * 2 + 1 - core},
            device_id_type=MESH,
        )

    def green_wait(block, part):
        index = block * 2 + core
        pltpu.make_async_copy(
            green.at[index, part], green.at[index, part], green_recv.at[index, part]
        ).wait()

    def green_step(step):
        for part in range(2):
            if step == 0:

                @pl.when(z < CHIPS - 1)
                def _():
                    green_copy(0, z, part, 0).start()

                @pl.when(z > 0)
                def _():
                    green_copy(0, z, part, 1).start()

                pair_copy(z, part).start()
            else:

                @pl.when(z >= step)
                def _():
                    green_wait(z - step, part)

                    @pl.when(z < CHIPS - 1)
                    def _():
                        green_copy(step, z - step, part, 0).start()

                    pair_copy(z - step, part).start()

                @pl.when(z + step < CHIPS)
                def _():
                    green_wait(z + step, part)

                    @pl.when(z > 0)
                    def _():
                        green_copy(step, z + step, part, 1).start()

                    pair_copy(z + step, part).start()

    def block_of(half, a, b, hh):
        return at(a, b, hh) if half == 0 else at(b, a, hh)

    def res_copy(half, a, b, hh, quarter, way):
        first = half * 256 + max(quarter, 0) * 128
        count = 256 if quarter < 0 else 128
        block = block_of(half, a, b, hh)
        da, db = way
        to = block_of(half, da, db, h)
        ref = res.at[block, pl.ds(first, count), :]
        return pltpu.make_async_remote_copy(
            src_ref=ref,
            dst_ref=ref,
            send_sem=res_send,
            recv_sem=res_recv.at[block, half * 2 + max(quarter, 0)],
            device_id={"src": to},
            device_id_type=MESH,
        )

    def res_wait(half, a, b, hh, quarter):
        first = half * 256 + max(quarter, 0) * 128
        count = 256 if quarter < 0 else 128
        block = block_of(half, a, b, hh)
        ref = res.at[block, pl.ds(first, count), :]
        pltpu.make_async_copy(ref, ref, res_recv.at[block, half * 2 + max(quarter, 0)]).wait()

    RIGHT, LEFT, UP, DOWN = (1, 0), (-1, 0), (0, 1), (0, -1)

    def res_round(step, hh):
        for half in range(2):
            if step == 0:
                res_copy(half, 0, 0, hh, -1, RIGHT).start()
                res_copy(half, 0, 0, hh, -1, LEFT).start()
            elif step == 1:
                res_wait(half, -1, 0, hh, -1)
                res_copy(half, -1, 0, hh, 0, RIGHT).start()
                res_wait(half, 1, 0, hh, -1)
                res_copy(half, 1, 0, hh, 1, LEFT).start()
            elif step == 2:
                res_wait(half, 2, 0, hh, 0)
                res_wait(half, 2, 0, hh, 1)
            elif step == 3:
                for a in (0, -1, 1):
                    res_wait(half, a, -1, hh, -1)
                    res_copy(half, a, -1, hh, 0, UP).start()
                    res_wait(half, a, 1, hh, -1)
                    res_copy(half, a, 1, hh, 1, DOWN).start()
            elif step == 4:
                res_wait(half, 2, -1, hh, -1)
                res_copy(half, 2, -1, hh, 0, UP).start()
                res_wait(half, 2, 1, hh, -1)
                res_copy(half, 2, 1, hh, 1, DOWN).start()
            else:
                for a in (0, -1, 1, 2):
                    res_wait(half, a, 2, hh, 0)
                    res_wait(half, a, 2, hh, 1)
        if step < 3:
            for half in range(2):
                for a in ((0,), (-1, 1), (2,))[step]:
                    res_copy(half, a, 0, hh, -1, UP).start()
                    res_copy(half, a, 0, hh, -1, DOWN).start()

    green_step(0)
    green_step(1)
    got[slab] = sent[slab]
    got_labels[slab] = sent_labels[slab]
    for d in range(1, SLABS):
        trace_wait(d)
    low_lanes = lax.broadcasted_iota(jnp.int32, (1, 128), 1) < CAP
    rows_f = lax.broadcasted_iota(jnp.int32, (ROWS, 128), 0).astype(jnp.float32)
    picks = []
    for i in range(SLABS // 2):
        row = jnp.where(low_lanes, got_labels[2 * i], got_labels[2 * i + 1])
        picks.append((rows_f == row).astype(jnp.float32).astype(jnp.bfloat16))
    assembled = jnp.dot(
        jnp.concatenate(picks, axis=1),
        got[...].reshape(SLABS * CAP, 128),
        preferred_element_type=jnp.float32,
    )
    res[src] = assembled.astype(jnp.bfloat16)

    twin_copy = pltpu.make_async_remote_copy(
        src_ref=res.at[src],
        dst_ref=res.at[src],
        send_sem=trace_send.at[0],
        recv_sem=trace_recv.at[SLABS],
        device_id={"src": twin},
        device_id_type=MESH,
    )
    twin_copy.start()
    res_round(0, h)
    green_step(2)
    res_round(1, h)
    res_round(2, h)
    green_step(3)
    res_round(3, h)
    pltpu.make_async_copy(res.at[twin], res.at[twin], trace_recv.at[SLABS]).wait()
    res_round(0, 1 - h)
    res_round(4, h)
    green_step(4)
    res_round(1, 1 - h)
    res_round(5, h)
    res_round(2, 1 - h)
    green_step(5)
    res_round(3, 1 - h)
    green_step(6)
    res_round(4, 1 - h)
    green_step(7)
    res_round(5, 1 - h)

    acc_re[...] = jnp.zeros_like(acc_re)
    acc_im[...] = jnp.zeros_like(acc_im)
    load_fields.wait()

    def multiply(block, carry):
        for part in range(2):
            other = block * 2 + 1 - core
            pltpu.make_async_copy(
                green.at[other, part], green.at[other, part], pair_recv.at[block, part]
            ).wait()
        for i in range(2):
            index = block * 2 + i
            left = jnp.concatenate([res[2 * index], res[2 * index + 1]], axis=1)
            g_re = green[index, 0]
            g_im = green[index, 1]
            half = CAP
            right_re = jnp.concatenate([g_re[:half], g_im[:half], g_re[half:], g_im[half:]], axis=0)
            right_im = jnp.concatenate(
                [g_im[:half], -g_re[:half], g_im[half:], -g_re[half:]], axis=0
            )
            acc_re[...] += jnp.dot(left, right_re, preferred_element_type=jnp.float32)
            acc_im[...] += jnp.dot(left, right_im, preferred_element_type=jnp.float32)
        return carry

    lax.fori_loop(0, CHIPS, multiply, 0)
    partial = jnp.sum(
        fields[0].astype(jnp.float32) * acc_re[...] - fields[1].astype(jnp.float32) * acc_im[...],
        axis=0,
        keepdims=True,
    )
    parts[slab] = partial

    def sum_copy(d):
        return pltpu.make_async_remote_copy(
            src_ref=parts.at[slab],
            dst_ref=parts.at[slab],
            send_sem=sum_send.at[d],
            recv_sem=sum_recv.at[slab],
            device_id={"slab": (slab + d) % SLABS},
            device_id_type=MESH,
        )

    for d in range(1, SLABS):
        sum_copy(d).start()

    for d in range(1, SLABS):
        for copy in trace_copy(d):
            copy.wait_send()
    twin_copy.wait_send()
    for part in range(2):
        for step in range(CHIPS):

            @pl.when((z >= step) & (z < CHIPS - 1))
            def _():
                green_copy(step, z, part, 0).wait_send()

            @pl.when((z + step < CHIPS) & (z > 0))
            def _():
                green_copy(step, z, part, 1).wait_send()

            pair_copy(step, part).wait_send()
    pltpu.make_async_copy(res.at[pl.ds(0, 30)], res.at[pl.ds(0, 30)], res_send).wait()

    for d in range(1, SLABS):
        frm = (slab + d) % SLABS
        pltpu.make_async_copy(parts.at[frm], parts.at[frm], sum_recv.at[frm]).wait()
    out_ref[...] = jnp.sum(parts[...], axis=0)
    for d in range(1, SLABS):
        sum_copy(d).wait_send()


def on_device(trace_values, trace_owner, trace_source, source_fields, green_fields):
    dma = pltpu.SemaphoreType.DMA
    vmem = pl.BlockSpec(memory_space=pltpu.VMEM)
    anyspace = pl.BlockSpec(memory_space=pltpu.HBM)
    out = pl.pallas_call(
        kernel,
        out_shape=jax.ShapeDtypeStruct((1, CELLS), jnp.float32),
        in_specs=[vmem, vmem, vmem, anyspace, anyspace],
        out_specs=vmem,
        scratch_shapes=[
            pltpu.VMEM((SLABS, CAP, 128), jnp.bfloat16),
            pltpu.VMEM((SLABS, 1, 128), jnp.float32),
            pltpu.VMEM((SLABS, CAP, 128), jnp.bfloat16),
            pltpu.VMEM((SLABS, 1, 128), jnp.float32),
            pltpu.VMEM((SRCS, ROWS, 128), jnp.bfloat16),
            pltpu.VMEM((SLABS, 2, 128, CELLS), jnp.bfloat16),
            pltpu.VMEM((2, ROWS, CELLS), jnp.bfloat16),
            pltpu.VMEM((ROWS, CELLS), jnp.float32),
            pltpu.VMEM((ROWS, CELLS), jnp.float32),
            pltpu.VMEM((SLABS, 1, CELLS), jnp.float32),
            dma((2,)),
            dma((SLABS,)),
            dma((SLABS + 1,)),
            dma((SLABS,)),
            dma((SLABS,)),
            dma((2, CHIPS, 2)),
            dma((SLABS, 2)),
            dma((CHIPS, 2)),
            dma((CHIPS, 2)),
            dma,
            dma((SRCS, 4)),
            dma((SLABS,)),
            dma((SLABS,)),
        ],
        compiler_params=pltpu.CompilerParams(
            collective_id=0, has_side_effects=True, vmem_limit_bytes=60 * 1024 * 1024
        ),
    )(
        trace_owner.reshape(1, ROWS),
        trace_source.reshape(1, ROWS),
        trace_values[0],
        source_fields,
        green_fields,
    )
    return out.reshape(CELLS)


def solution(mesh):
    in_specs = (
        P("src", "slab", None),
        P("src", "slab", None),
        P("src", "slab"),
        P(None, "slab", "src"),
        P(None, "slab", "src"),
    )
    return jax.shard_map(
        on_device, mesh=mesh, in_specs=in_specs, out_specs=P("src"), check_vma=False
    )
```

```python
import jax
import jax.numpy as jnp
from jax import lax
from jax.experimental import pallas as pl
from jax.experimental.pallas import tpu as pltpu
from jax.sharding import PartitionSpec as P

MESH = pl.DeviceIdType.MESH
SLABS = 16
SRCS = 32
CAP = 64
ROWS = 512
CELLS = 512
CHIPS = 8
RING = 16
EARLY_STEPS = 5


def kernel(
    owner_hbm,
    label_hbm,
    values_hbm,
    fields_hbm,
    green_hbm,
    out_ref,
    owner_ref,
    label_ref,
    values_ref,
    sent,
    sent_labels,
    got,
    got_labels,
    res,
    green,
    fields,
    acc_re,
    acc_im,
    parts,
    load_sem,
    trace_sem,
    green_send,
    green_recv,
    pair_send,
    pair_recv,
    twin_sem,
    res_send,
    res_recv,
    sum_sem,
    from_left,
    from_right,
):
    slab = lax.axis_index("slab")
    src = lax.axis_index("src")
    z, core = slab // 2, slab % 2
    y, x, h = src // 8, (src // 2) % 4, src % 2
    ring = h * CHIPS + z

    loads = []
    for i, (a, b) in enumerate(
        (
            (owner_hbm, owner_ref),
            (label_hbm, label_ref),
            (values_hbm, values_ref),
            (green_hbm, green.at[slab]),
            (fields_hbm, fields),
        )
    ):
        loads.append(pltpu.make_async_copy(a, b, load_sem.at[i]))
        loads[-1].start()

    def at(dx, dy, hh):
        return (((y + dy + 4) % 4) * 4 + (x + dx + 4) % 4) * 2 + hh

    def along(d, to_core=core):
        to = (ring + d + RING) % RING
        return {"slab": (to % CHIPS) * 2 + to_core, "src": src - h + to // CHIPS}

    barrier = pltpu.get_barrier_semaphore()
    neighbours = [along(1), along(-1), {"slab": z * 2 + 1 - core}]
    neighbours += [along(1, 1 - core), along(-1, 1 - core)]
    neighbours += [{"src": at(1, 0, h)}, {"src": at(-1, 0, h)}]
    neighbours += [{"src": at(0, 1, h)}, {"src": at(0, -1, h)}]
    for other in neighbours:
        pl.semaphore_signal(barrier, inc=1, device_id=other, device_id_type=MESH)

    loads[0].wait()
    loads[1].wait()
    owners = owner_ref[...]
    labels = label_ref[...]
    hits = lax.broadcasted_iota(jnp.int32, (SLABS, ROWS), 0) == owners
    hits_f = hits.astype(jnp.float32)
    earlier = lax.broadcasted_iota(jnp.int32, (ROWS, ROWS), 0) < lax.broadcasted_iota(
        jnp.int32, (ROWS, ROWS), 1
    )
    counts = jnp.dot(
        hits_f.astype(jnp.bfloat16),
        earlier.astype(jnp.float32).astype(jnp.bfloat16),
        preferred_element_type=jnp.float32,
    )
    ranks = jnp.sum(counts * hits_f, axis=0, keepdims=True).astype(jnp.int32)
    slots = owners * CAP + ranks
    placing = (
        (lax.broadcasted_iota(jnp.int32, (SLABS * CAP, ROWS), 0) == slots)
        .astype(jnp.float32)
        .astype(jnp.bfloat16)
    )
    rank_hits = (
        (lax.broadcasted_iota(jnp.int32, (128, ROWS), 0) % CAP == ranks)
        .astype(jnp.float32)
        .astype(jnp.bfloat16)
    )
    high = (labels // 32).astype(jnp.float32)
    low = (labels % 32 + 1).astype(jnp.float32)
    codes = jnp.concatenate([hits_f * high, hits_f * low], axis=0).astype(jnp.bfloat16)
    placed_codes = lax.dot_general(
        codes, rank_hits, (((1,), (1,)), ((), ())), preferred_element_type=jnp.float32
    )
    label_rows = placed_codes[:SLABS] * 32.0 + placed_codes[SLABS:] - 1.0
    for k in range(SLABS):
        sent_labels[k] = label_rows[k : k + 1, :]
    loads[2].wait()
    placed = jnp.dot(placing, values_ref[...], preferred_element_type=jnp.float32)
    sent[...] = placed.astype(jnp.bfloat16).reshape(SLABS, CAP, 128)

    def green_copy(block, part, d):
        ref = green.at[block * 2 + core, part]
        return pltpu.make_async_remote_copy(
            src_ref=ref,
            dst_ref=ref,
            send_sem=green_send,
            recv_sem=green_recv.at[block, part],
            device_id={"slab": slab + 2 * d},
            device_id_type=MESH,
        )

    def pair_copy(block, part):
        ref = green.at[block * 2 + core, part]
        return pltpu.make_async_remote_copy(
            src_ref=ref,
            dst_ref=ref,
            send_sem=pair_send,
            recv_sem=pair_recv.at[block],
            device_id={"slab": z * 2 + 1 - core},
            device_id_type=MESH,
        )

    def green_wait(block, part):
        ref = green.at[block * 2 + core, part]
        pltpu.make_async_copy(ref, ref, green_recv.at[block, part]).wait()

    def green_start():
        for part in range(2):

            @pl.when(z < CHIPS - 1)
            def _():
                green_copy(z, part, 1).start()

            @pl.when(z > 0)
            def _():
                green_copy(z, part, -1).start()

        for part in range(2):
            pair_copy(z, part).start()

    def green_step(step):
        for part in range(2):

            @pl.when(z >= step)
            def _():
                green_wait(z - step, part)

                @pl.when(z < CHIPS - 1)
                def _():
                    green_copy(z - step, part, 1).start()

                pair_copy(z - step, part).start()

            @pl.when(z + step < CHIPS)
            def _():
                green_wait(z + step, part)

                @pl.when(z > 0)
                def _():
                    green_copy(z + step, part, -1).start()

                pair_copy(z + step, part).start()

    def trace_send(to):
        pltpu.make_async_remote_copy(
            src_ref=sent.at[to],
            dst_ref=got.at[slab],
            send_sem=trace_sem.at[0],
            recv_sem=trace_sem.at[1],
            device_id={"slab": to},
            device_id_type=MESH,
        ).start()
        pltpu.make_async_remote_copy(
            src_ref=sent_labels.at[to],
            dst_ref=got_labels.at[slab],
            send_sem=trace_sem.at[2],
            recv_sem=trace_sem.at[3],
            device_id={"slab": to},
            device_id_type=MESH,
        ).start()

    def all_traces(i):
        ref = (got, got_labels)[i // 2].at[pl.ds(0, SLABS - 1)]
        pltpu.make_async_copy(ref, ref, trace_sem.at[i]).wait()

    def trace_steps():
        for s in range(1, CHIPS + 1):
            if s > 1:
                pl.semaphore_wait(from_left.at[s - 2], 1)
            if s < CHIPS:
                pl.semaphore_signal(
                    from_left.at[s - 1], inc=1, device_id=along(1), device_id_type=MESH
                )

                @pl.when(z >= s)
                def _():
                    for other in range(2):
                        trace_send((z - s) * 2 + other)

                @pl.when(z + s < CHIPS)
                def _():
                    if s > 1:
                        pl.semaphore_wait(from_right.at[s - 2], 1)

                    @pl.when(z > 0)
                    def _():
                        pl.semaphore_signal(
                            from_right.at[s - 1], inc=1, device_id=along(-1), device_id_type=MESH
                        )

                    for other in range(2):
                        trace_send((z + s) * 2 + other)

    def block_of(half, a, b, hh):
        return at(a, b, hh) if half == 0 else at(b, a, hh)

    def res_copy(half, a, b, hh, quarter, way, sem):
        first = half * 256 + max(quarter, 0) * 128
        ref = res.at[block_of(half, a, b, hh), pl.ds(first, 256 if quarter < 0 else 128), :]
        pltpu.make_async_remote_copy(
            src_ref=ref,
            dst_ref=ref,
            send_sem=res_send,
            recv_sem=res_recv.at[sem],
            device_id={"src": block_of(half, way[0], way[1], h)},
            device_id_type=MESH,
        ).start()

    RIGHT, LEFT, UP, DOWN = (1, 0), (-1, 0), (0, 1), (0, -1)

    def res_round(step, turn):
        hh = (h, 1 - h)[turn]
        for half in range(2):

            def sem(number):
                return (turn * 5 + number - 1) * 2 + half

            if step > 0:
                ref = (
                    res.at[0],
                    res.at[0, pl.ds(0, 256), :],
                    res.at[pl.ds(0, 3)],
                    res.at[0],
                    res.at[pl.ds(0, 2)],
                )[step - 1]
                pltpu.make_async_copy(ref, ref, res_recv.at[sem(step)]).wait()
            if step == 0:
                res_copy(half, 0, 0, hh, -1, RIGHT, sem(1))
                res_copy(half, 0, 0, hh, -1, LEFT, sem(1))
            elif step == 1:
                res_copy(half, -1, 0, hh, 0, RIGHT, sem(2))
                res_copy(half, 1, 0, hh, 1, LEFT, sem(2))
            elif step == 3:
                for a in (0, -1, 1):
                    res_copy(half, a, -1, hh, 0, UP, sem(5))
                    res_copy(half, a, 1, hh, 1, DOWN, sem(5))
            elif step == 4:
                res_copy(half, 2, -1, hh, 0, UP, sem(5))
                res_copy(half, 2, 1, hh, 1, DOWN, sem(5))
        if step < 3:
            for half in range(2):
                number = (turn * 5 + (3 if step < 2 else 4) - 1) * 2 + half
                for a in ((0,), (-1, 1), (2,))[step]:
                    res_copy(half, a, 0, hh, -1, UP, number)
                    res_copy(half, a, 0, hh, -1, DOWN, number)

    loads[3].wait()
    pl.semaphore_wait(barrier, len(neighbours))
    late = (ring >= 6) & (ring < 10)

    @pl.when(jnp.logical_not(late))
    def _():
        green_start()

    trace_send(z * 2 + 1 - core)
    trace_steps()

    @pl.when(late)
    def _():
        green_start()

    got[slab] = sent[slab]
    got_labels[slab] = sent_labels[slab]
    green_step(1)
    all_traces(1)
    all_traces(3)
    low_lanes = lax.broadcasted_iota(jnp.int32, (1, 128), 1) < CAP
    rows_f = lax.broadcasted_iota(jnp.int32, (ROWS, 128), 0).astype(jnp.float32)
    picks = []
    for i in range(SLABS // 2):
        row = jnp.where(low_lanes, got_labels[2 * i], got_labels[2 * i + 1])
        picks.append((rows_f == row).astype(jnp.float32).astype(jnp.bfloat16))
    assembled = jnp.dot(
        jnp.concatenate(picks, axis=1),
        got[...].reshape(SLABS * CAP, 128),
        preferred_element_type=jnp.float32,
    )
    res[src] = assembled.astype(jnp.bfloat16)

    twin = at(0, 0, 1 - h)
    twin_copy = pltpu.make_async_remote_copy(
        src_ref=res.at[src],
        dst_ref=res.at[src],
        send_sem=twin_sem.at[0],
        recv_sem=twin_sem.at[1],
        device_id={"src": twin},
        device_id_type=MESH,
    )
    twin_copy.start()
    res_round(0, 0)
    green_step(2)
    res_round(1, 0)
    res_round(2, 0)
    green_step(3)
    res_round(3, 0)
    res_round(4, 0)
    pltpu.make_async_copy(res.at[twin], res.at[twin], twin_sem.at[1]).wait()
    res_round(0, 1)
    res_round(5, 0)
    green_step(4)
    res_round(1, 1)
    res_round(2, 1)
    green_step(5)
    acc_re[...] = jnp.zeros_like(acc_re)
    acc_im[...] = jnp.zeros_like(acc_im)
    loads[4].wait()
    res_round(3, 1)
    res_round(4, 1)
    res_round(5, 1)

    def chip_of(n):
        m = jnp.minimum(z, CHIPS - 1 - z)
        side = z + jnp.where(n % 2 == 1, -((n + 1) // 2), n // 2)
        rest = jnp.where(z < CHIPS // 2, n, CHIPS - 1 - n)
        return jnp.where(n <= 2 * m, side, rest)

    def multiply(n, carry):
        block = chip_of(n)
        far = jnp.abs(block - z)
        before = jnp.abs(chip_of(jnp.maximum(n - 1, 0)) - z)

        @pl.when((far > EARLY_STEPS) & (far > before))
        def _():
            green_step(far)

        ref = green.at[block * 2 + 1 - core]
        pltpu.make_async_copy(ref, ref, pair_recv.at[block]).wait()
        for i in range(2):
            index = block * 2 + i
            left = jnp.concatenate([res[2 * index], res[2 * index + 1]], axis=1)
            g_re = green[index, 0]
            g_im = green[index, 1]
            right_re = jnp.concatenate([g_re[:CAP], g_im[:CAP], g_re[CAP:], g_im[CAP:]], axis=0)
            right_im = jnp.concatenate([g_im[:CAP], -g_re[:CAP], g_im[CAP:], -g_re[CAP:]], axis=0)
            acc_re[...] += jnp.dot(left, right_re, preferred_element_type=jnp.float32)
            acc_im[...] += jnp.dot(left, right_im, preferred_element_type=jnp.float32)
        return carry

    lax.fori_loop(0, CHIPS, multiply, 0)
    partial = jnp.sum(
        fields[0].astype(jnp.float32) * acc_re[...] - fields[1].astype(jnp.float32) * acc_im[...],
        axis=0,
        keepdims=True,
    )
    parts[slab] = partial
    for d in range(1, SLABS):
        pltpu.make_async_remote_copy(
            src_ref=parts.at[slab],
            dst_ref=parts.at[slab],
            send_sem=sum_sem.at[0],
            recv_sem=sum_sem.at[1],
            device_id={"slab": (slab + d) % SLABS},
            device_id_type=MESH,
        ).start()

    all_traces(0)
    all_traces(2)
    twin_copy.wait_send()
    end = (z == 0) | (z == CHIPS - 1)

    @pl.when(end)
    def _():
        pltpu.make_async_copy(green.at[0], green.at[0], green_send).wait()

    @pl.when(jnp.logical_not(end))
    def _():
        ref = green.at[pl.ds(0, CHIPS + 1)]
        pltpu.make_async_copy(ref, ref, green_send).wait()

    ref = green.at[pl.ds(0, CHIPS)]
    pltpu.make_async_copy(ref, ref, pair_send).wait()
    ref = res.at[pl.ds(0, SRCS - 2)]
    pltpu.make_async_copy(ref, ref, res_send).wait()

    ref = parts.at[pl.ds(0, SLABS - 1)]
    pltpu.make_async_copy(ref, ref, sum_sem.at[1]).wait()
    out_ref[...] = jnp.sum(parts[...], axis=0)
    pltpu.make_async_copy(ref, ref, sum_sem.at[0]).wait()


def on_device(trace_values, trace_owner, trace_source, source_fields, green_fields):
    dma = pltpu.SemaphoreType.DMA
    out = pl.pallas_call(
        kernel,
        out_shape=jax.ShapeDtypeStruct((1, CELLS), jnp.float32),
        in_specs=[pl.BlockSpec(memory_space=pltpu.HBM)] * 5,
        out_specs=pl.BlockSpec(memory_space=pltpu.VMEM),
        scratch_shapes=[
            pltpu.VMEM((1, ROWS), jnp.int32),
            pltpu.VMEM((1, ROWS), jnp.int32),
            pltpu.VMEM((ROWS, 128), jnp.bfloat16),
            pltpu.VMEM((SLABS, CAP, 128), jnp.bfloat16),
            pltpu.VMEM((SLABS, 1, 128), jnp.float32),
            pltpu.VMEM((SLABS, CAP, 128), jnp.bfloat16),
            pltpu.VMEM((SLABS, 1, 128), jnp.float32),
            pltpu.VMEM((SRCS, ROWS, 128), jnp.bfloat16),
            pltpu.VMEM((SLABS, 2, 128, CELLS), jnp.bfloat16),
            pltpu.VMEM((2, ROWS, CELLS), jnp.bfloat16),
            pltpu.VMEM((ROWS, CELLS), jnp.float32),
            pltpu.VMEM((ROWS, CELLS), jnp.float32),
            pltpu.VMEM((SLABS, 1, CELLS), jnp.float32),
            dma((5,)),
            dma((4,)),
            dma,
            dma((CHIPS, 2)),
            dma,
            dma((CHIPS,)),
            dma((2,)),
            dma,
            dma((20,)),
            dma((2,)),
            pltpu.SemaphoreType.REGULAR((CHIPS - 1,)),
            pltpu.SemaphoreType.REGULAR((CHIPS - 1,)),
        ],
        compiler_params=pltpu.CompilerParams(
            collective_id=0, has_side_effects=True, vmem_limit_bytes=60 * 1024 * 1024
        ),
    )(
        trace_owner.reshape(1, ROWS),
        trace_source.reshape(1, ROWS),
        trace_values[0],
        source_fields,
        green_fields,
    )
    return out.reshape(CELLS)


def solution(mesh):
    in_specs = (
        P("src", "slab", None),
        P("src", "slab", None),
        P("src", "slab"),
        P(None, "slab", "src"),
        P(None, "slab", "src"),
    )
    return jax.shard_map(
        on_device, mesh=mesh, in_specs=in_specs, out_specs=P("src"), check_vma=False
    )
```

```python
import jax
import jax.numpy as jnp
from jax import lax
from jax.experimental import pallas as pl
from jax.experimental.pallas import tpu as pltpu
from jax.sharding import PartitionSpec as P

MESH = pl.DeviceIdType.MESH
SLABS = 16
SRCS = 32
CAP = 64
ROWS = 512
CELLS = 512
CHIPS = 8
RING = 16
EARLY_STEPS = 6


def kernel(
    owner_hbm,
    label_hbm,
    values_hbm,
    fields_hbm,
    green_hbm,
    out_ref,
    owner_ref,
    label_ref,
    values_ref,
    sent,
    sent_labels,
    got,
    got_labels,
    res,
    green,
    fields,
    acc_re,
    acc_im,
    parts,
    load_sem,
    hand_sem,
    trace_sem,
    green_send,
    green_recv,
    pair_send,
    pair_recv,
    own_sem,
    twin_sem,
    res_send,
    res_recv,
    give_send,
    give_recv,
    sum_sem,
    from_left,
    from_right,
    across,
):
    slab = lax.axis_index("slab")
    src = lax.axis_index("src")
    z, core = slab // 2, slab % 2
    y, x, h = src // 8, (src // 2) % 4, src % 2
    ring = h * CHIPS + z

    loads = []
    for i, (a, b) in enumerate(
        (
            (owner_hbm, owner_ref),
            (label_hbm, label_ref),
            (values_hbm, values_ref),
            (green_hbm, green.at[slab]),
            (fields_hbm, fields),
        )
    ):
        loads.append(pltpu.make_async_copy(a, b, load_sem.at[i]))
        loads[-1].start()

    def at(dx, dy, hh):
        return (((y + dy + 4) % 4) * 4 + (x + dx + 4) % 4) * 2 + hh

    def along(d, to_core=core):
        to = (ring + d + RING) % RING
        return {"slab": (to % CHIPS) * 2 + to_core, "src": src - h + to // CHIPS}

    barrier = pltpu.get_barrier_semaphore()
    neighbours = [along(1), along(-1), {"slab": z * 2 + 1 - core}]
    neighbours += [along(1, 1 - core), along(-1, 1 - core)]
    neighbours += [{"src": at(1, 0, h)}, {"src": at(-1, 0, h)}]
    neighbours += [{"src": at(0, 1, h)}, {"src": at(0, -1, h)}]
    for other in neighbours:
        pl.semaphore_signal(barrier, inc=1, device_id=other, device_id_type=MESH)

    loads[0].wait()
    loads[1].wait()
    owners = owner_ref[...]
    labels = label_ref[...]
    hits = lax.broadcasted_iota(jnp.int32, (SLABS, ROWS), 0) == owners
    hits_f = hits.astype(jnp.float32)
    earlier = lax.broadcasted_iota(jnp.int32, (ROWS, ROWS), 0) < lax.broadcasted_iota(
        jnp.int32, (ROWS, ROWS), 1
    )
    counts = jnp.dot(
        hits_f.astype(jnp.bfloat16),
        earlier.astype(jnp.float32).astype(jnp.bfloat16),
        preferred_element_type=jnp.float32,
    )
    ranks = jnp.sum(counts * hits_f, axis=0, keepdims=True).astype(jnp.int32)
    slots = owners * CAP + ranks
    placing = (
        (lax.broadcasted_iota(jnp.int32, (SLABS * CAP, ROWS), 0) == slots)
        .astype(jnp.float32)
        .astype(jnp.bfloat16)
    )
    rank_hits = (
        (lax.broadcasted_iota(jnp.int32, (128, ROWS), 0) % CAP == ranks)
        .astype(jnp.float32)
        .astype(jnp.bfloat16)
    )
    high = (labels // 32).astype(jnp.float32)
    low = (labels % 32 + 1).astype(jnp.float32)
    codes = jnp.concatenate([hits_f * high, hits_f * low], axis=0).astype(jnp.bfloat16)
    placed_codes = lax.dot_general(
        codes, rank_hits, (((1,), (1,)), ((), ())), preferred_element_type=jnp.float32
    )
    label_rows = placed_codes[:SLABS] * 32.0 + placed_codes[SLABS:] - 1.0
    for k in range(SLABS):
        sent_labels[core, k] = label_rows[k : k + 1, :]
    loads[2].wait()
    placed = jnp.dot(placing, values_ref[...], preferred_element_type=jnp.float32)
    sent[core] = placed.astype(jnp.bfloat16).reshape(SLABS, CAP, 128)

    def remote(src_ref, dst_ref, send_sem, recv_sem, to):
        return pltpu.make_async_remote_copy(
            src_ref=src_ref,
            dst_ref=dst_ref,
            send_sem=send_sem,
            recv_sem=recv_sem,
            device_id=to,
            device_id_type=MESH,
        )

    def arrived(ref, sem):
        pltpu.make_async_copy(ref, ref, sem).wait()

    partner = {"slab": z * 2 + 1 - core}
    hand_values = remote(sent.at[0], sent.at[0], hand_sem.at[0], hand_sem.at[1], partner)
    hand_labels = remote(
        sent_labels.at[0], sent_labels.at[0], hand_sem.at[2], hand_sem.at[3], partner
    )
    own_block = green.at[z * 2 + 1]
    own_copy = remote(own_block, own_block, own_sem.at[0], own_sem.at[1], partner)

    def green_copy(block, piece, d):
        ref = green.at[block * 2 + piece // 2, piece % 2]
        return remote(ref, ref, green_send, green_recv.at[block, piece], {"slab": slab + 2 * d})

    def pair_copy(block, piece):
        ref = green.at[block * 2 + piece // 2, piece % 2]
        return remote(ref, ref, pair_send, pair_recv.at[block], partner)

    def green_wait(block, piece):
        arrived(green.at[block * 2 + piece // 2, piece % 2], green_recv.at[block, piece])

    def green_start(piece):
        @pl.when(z < CHIPS - 1)
        def _():
            green_copy(z, piece, 1).start()

        @pl.when(z > 0)
        def _():
            green_copy(z, piece, -1).start()

    def green_step(step):
        for piece in range(4):

            @pl.when(z >= step)
            def _():
                green_wait(z - step, piece)

                @pl.when(z < CHIPS - 1)
                def _():
                    green_copy(z - step, piece, 1).start()

                pair_copy(z - step, piece).start()

            @pl.when(z + step < CHIPS)
            def _():
                green_wait(z + step, piece)

                @pl.when(z > 0)
                def _():
                    green_copy(z + step, piece, -1).start()

                pair_copy(z + step, piece).start()

    def trace_send(chip):
        to = {"slab": chip * 2 + core}
        owners_of = pl.ds(chip * 2, 2)
        remote(sent.at[:, owners_of], got.at[z], trace_sem.at[0], trace_sem.at[1], to).start()
        remote(
            sent_labels.at[:, owners_of], got_labels.at[z], trace_sem.at[2], trace_sem.at[3], to
        ).start()

    def all_traces(i):
        arrived((got, got_labels)[i // 2].at[pl.ds(0, CHIPS - 1)], trace_sem.at[i])

    def trace_steps(first, last):
        for s in range(first, last + 1):

            @pl.when(z >= s)
            def _():
                if s > 1:
                    pl.semaphore_wait(from_left.at[s - 2], 1)

                @pl.when(z < CHIPS - 1)
                def _():
                    pl.semaphore_signal(
                        from_left.at[s - 1], inc=1, device_id=along(1), device_id_type=MESH
                    )

                trace_send(z - s)

            @pl.when(z + s < CHIPS)
            def _():
                if s > 1:
                    pl.semaphore_wait(from_right.at[s - 2], 1)

                @pl.when(z > 0)
                def _():
                    pl.semaphore_signal(
                        from_right.at[s - 1], inc=1, device_id=along(-1), device_id_type=MESH
                    )

                trace_send(z + s)

    gap = jnp.where(h == 0, CHIPS - 1 - z, z)
    inward = 1 - 2 * h

    def other_line():
        pl.semaphore_wait(across, 1)

        @pl.when(gap < CHIPS - 1)
        def _():
            pl.semaphore_signal(across, inc=1, device_id=along(-inward), device_id_type=MESH)

    def block_of(half, a, b, hh):
        return at(a, b, hh) if half == 0 else at(b, a, hh)

    def res_copy(half, a, b, hh, quarter, way, sem):
        first = half * ROWS + max(quarter, 0) * (ROWS // 2)
        count = ROWS if quarter < 0 else ROWS // 2
        ref = res.at[block_of(half, a, b, hh), pl.ds(first, count), :]
        to = {"src": block_of(half, way[0], way[1], h)}
        remote(ref, ref, res_send, res_recv.at[sem], to).start()

    def give(turn, a, b):
        ref = res.at[at(a, b, (h, 1 - h)[turn]), pl.ds(0, ROWS), :]
        remote(ref, ref, give_send, give_recv.at[turn], partner).start()

    RIGHT, LEFT, UP, DOWN = (1, 0), (-1, 0), (0, 1), (0, -1)

    def res_round(step, turn):
        hh = (h, 1 - h)[turn]
        for half in range(2):

            def sem(number):
                return (turn * 5 + number - 1) * 2 + half

            if step > 0:
                ref = (
                    res.at[0],
                    res.at[0, pl.ds(0, ROWS), :],
                    res.at[pl.ds(0, 3)],
                    res.at[0],
                    res.at[pl.ds(0, 2)],
                )[step - 1]
                arrived(ref, res_recv.at[sem(step)])
            if step == 0:
                res_copy(half, 0, 0, hh, -1, RIGHT, sem(1))
                res_copy(half, 0, 0, hh, -1, LEFT, sem(1))
            elif step == 1:
                res_copy(half, -1, 0, hh, 0, RIGHT, sem(2))
                res_copy(half, 1, 0, hh, 1, LEFT, sem(2))
            elif step == 3:
                for a in (0, -1, 1):
                    res_copy(half, a, -1, hh, 0, UP, sem(5))
                    res_copy(half, a, 1, hh, 1, DOWN, sem(5))
            elif step == 4:
                res_copy(half, 2, -1, hh, 0, UP, sem(5))
                res_copy(half, 2, 1, hh, 1, DOWN, sem(5))
        if step < 3:
            for half in range(2):
                number = (turn * 5 + (3 if step < 2 else 4) - 1) * 2 + half
                for a in ((0,), (-1, 1), (2,))[step]:
                    res_copy(half, a, 0, hh, -1, UP, number)
                    res_copy(half, a, 0, hh, -1, DOWN, number)
        for a, b in (
            ((0, 0),),
            ((-1, 0), (1, 0)),
            ((2, 0),),
            ((0, -1), (0, 1), (-1, -1), (-1, 1), (1, -1), (1, 1)),
            ((2, -1), (2, 1)),
            ((0, 2), (-1, 2), (1, 2), (2, 2)),
        )[step]:
            give(turn, a, b)

    loads[3].wait()
    pl.semaphore_wait(barrier, len(neighbours))

    @pl.when(core == 0)
    def _():
        hand_labels.start()
        hand_values.start()
        for piece in range(2):
            green_start(piece)
        arrived(own_block, own_sem.at[1])
        for piece in range(2, 4):
            green_start(piece)
        for piece in range(2):
            pair_copy(z, piece).start()
        for step in range(1, EARLY_STEPS + 1):
            green_step(step)
        for turn in range(2):
            arrived(res.at[pl.ds(0, SRCS // 4)], give_recv.at[turn])

    @pl.when(core == 1)
    def _():
        own_copy.start()
        arrived(sent_labels.at[0], hand_sem.at[3])
        arrived(sent.at[0], hand_sem.at[1])
        trace_steps(1, CHIPS - 1)
        for i in range(2):
            got[z, i] = sent[i, pl.ds(z * 2, 2)]
            got_labels[z, i] = sent_labels[i, pl.ds(z * 2, 2)]

        @pl.when(gap == 0)
        def _():
            pl.semaphore_signal(across, inc=1, device_id=along(inward), device_id_type=MESH)

        @pl.when(gap <= 4)
        def _():
            other_line()

        all_traces(3)
        all_traces(1)

        @pl.when(gap > 4)
        def _():
            other_line()

        low_lanes = lax.broadcasted_iota(jnp.int32, (1, 128), 1) < CAP
        rows_f = lax.broadcasted_iota(jnp.int32, (ROWS, 128), 0).astype(jnp.float32)
        for owner in range(2):
            picks = []
            for chip in range(CHIPS):
                row = jnp.where(low_lanes, got_labels[chip, 0, owner], got_labels[chip, 1, owner])
                picks.append((rows_f == row).astype(jnp.float32).astype(jnp.bfloat16))
            assembled = jnp.dot(
                jnp.concatenate(picks, axis=1),
                got[:, :, owner].reshape(SLABS * CAP, 128),
                preferred_element_type=jnp.float32,
            )
            res[src, pl.ds(owner * ROWS, ROWS), :] = assembled.astype(jnp.bfloat16)

        twin = at(0, 0, 1 - h)
        twin_copy = remote(
            res.at[src], res.at[src], twin_sem.at[0], twin_sem.at[1], {"src": twin}
        )
        twin_copy.start()
        for step in range(5):
            res_round(step, 0)
        arrived(res.at[twin], twin_sem.at[1])
        res_round(0, 1)
        res_round(5, 0)
        for step in range(1, 6):
            res_round(step, 1)
        twin_copy.wait_send()

    acc_re[...] = jnp.zeros_like(acc_re)
    acc_im[...] = jnp.zeros_like(acc_im)
    loads[4].wait()

    def chip_of(n):
        m = jnp.minimum(z, CHIPS - 1 - z)
        side = z + jnp.where(n % 2 == 1, -((n + 1) // 2), n // 2)
        rest = jnp.where(z < CHIPS // 2, n, CHIPS - 1 - n)
        return jnp.where(n <= 2 * m, side, rest)

    def multiply(n, carry):
        block = chip_of(n)
        far = jnp.abs(block - z)
        before = jnp.abs(chip_of(jnp.maximum(n - 1, 0)) - z)

        @pl.when((core == 0) & (far > EARLY_STEPS) & (far > before))
        def _():
            green_step(far)

        @pl.when((core == 1) & (far == 0))
        def _():
            arrived(green.at[0], pair_recv.at[block])

        @pl.when((core == 1) & (far > 0))
        def _():
            arrived(green.at[pl.ds(0, 2)], pair_recv.at[block])

        for i in range(2):
            index = block * 2 + i
            rows = pl.ds(pl.multiple_of(core * ROWS, ROWS), ROWS)
            left = jnp.concatenate([res[2 * index, rows, :], res[2 * index + 1, rows, :]], axis=1)
            g_re = green[index, 0]
            g_im = green[index, 1]
            right_re = jnp.concatenate([g_re[:CAP], g_im[:CAP], g_re[CAP:], g_im[CAP:]], axis=0)
            right_im = jnp.concatenate([g_im[:CAP], -g_re[:CAP], g_im[CAP:], -g_re[CAP:]], axis=0)
            acc_re[...] += jnp.dot(left, right_re, preferred_element_type=jnp.float32)
            acc_im[...] += jnp.dot(left, right_im, preferred_element_type=jnp.float32)
        return carry

    lax.fori_loop(0, CHIPS, multiply, 0)
    partial = jnp.sum(
        fields[0].astype(jnp.float32) * acc_re[...] - fields[1].astype(jnp.float32) * acc_im[...],
        axis=0,
        keepdims=True,
    )
    parts[slab] = partial
    for d in range(1, SLABS):
        to = {"slab": (slab + d) % SLABS}
        remote(parts.at[slab], parts.at[slab], sum_sem.at[0], sum_sem.at[1], to).start()

    end = (z == 0) | (z == CHIPS - 1)

    @pl.when(core == 0)
    def _():
        hand_values.wait_send()
        hand_labels.wait_send()
        arrived(green.at[pl.ds(0, SLABS - 1)], pair_send)

        @pl.when(end)
        def _():
            arrived(res.at[pl.ds(0, 2)], green_send)

        @pl.when(jnp.logical_not(end))
        def _():
            arrived(res.at[pl.ds(0, 2 * CHIPS + 2)], green_send)

    @pl.when(core == 1)
    def _():
        own_copy.wait_send()
        all_traces(0)
        all_traces(2)
        arrived(res.at[pl.ds(0, SRCS - 2)], res_send)
        arrived(res.at[pl.ds(0, SRCS // 2)], give_send)

    arrived(parts.at[pl.ds(0, SLABS - 1)], sum_sem.at[1])
    out_ref[...] = jnp.sum(parts[...], axis=0)
    arrived(parts.at[pl.ds(0, SLABS - 1)], sum_sem.at[0])


def on_device(trace_values, trace_owner, trace_source, source_fields, green_fields):
    dma = pltpu.SemaphoreType.DMA
    out = pl.pallas_call(
        kernel,
        out_shape=jax.ShapeDtypeStruct((1, CELLS), jnp.float32),
        in_specs=[pl.BlockSpec(memory_space=pltpu.HBM)] * 5,
        out_specs=pl.BlockSpec(memory_space=pltpu.VMEM),
        scratch_shapes=[
            pltpu.VMEM((1, ROWS), jnp.int32),
            pltpu.VMEM((1, ROWS), jnp.int32),
            pltpu.VMEM((ROWS, 128), jnp.bfloat16),
            pltpu.VMEM((2, SLABS, CAP, 128), jnp.bfloat16),
            pltpu.VMEM((2, SLABS, 1, 128), jnp.float32),
            pltpu.VMEM((CHIPS, 2, 2, CAP, 128), jnp.bfloat16),
            pltpu.VMEM((CHIPS, 2, 2, 1, 128), jnp.float32),
            pltpu.VMEM((SRCS, 2 * ROWS, 128), jnp.bfloat16),
            pltpu.VMEM((SLABS, 2, 128, CELLS), jnp.bfloat16),
            pltpu.VMEM((2, ROWS, CELLS), jnp.bfloat16),
            pltpu.VMEM((ROWS, CELLS), jnp.float32),
            pltpu.VMEM((ROWS, CELLS), jnp.float32),
            pltpu.VMEM((SLABS, 1, CELLS), jnp.float32),
            dma((5,)),
            dma((4,)),
            dma((4,)),
            dma,
            dma((CHIPS, 4)),
            dma,
            dma((CHIPS,)),
            dma((2,)),
            dma((2,)),
            dma,
            dma((20,)),
            dma,
            dma((2,)),
            dma((2,)),
            pltpu.SemaphoreType.REGULAR((CHIPS - 1,)),
            pltpu.SemaphoreType.REGULAR((CHIPS - 1,)),
            pltpu.SemaphoreType.REGULAR,
        ],
        compiler_params=pltpu.CompilerParams(
            collective_id=0, has_side_effects=True, vmem_limit_bytes=60 * 1024 * 1024
        ),
    )(
        trace_owner.reshape(1, ROWS),
        trace_source.reshape(1, ROWS),
        trace_values[0],
        source_fields,
        green_fields,
    )
    return out.reshape(CELLS)


def solution(mesh):
    in_specs = (
        P("src", "slab", None),
        P("src", "slab", None),
        P("src", "slab"),
        P(None, "slab", "src"),
        P(None, "slab", "src"),
    )
    return jax.shard_map(
        on_device, mesh=mesh, in_specs=in_specs, out_specs=P("src"), check_vma=False
    )
```

```python
import jax
import jax.numpy as jnp
from jax import lax
from jax.experimental import pallas as pl
from jax.experimental.pallas import tpu as pltpu
from jax.sharding import PartitionSpec as P

MESH = pl.DeviceIdType.MESH
SLABS = 16
SRCS = 32
CAP = 64
ROWS = 512
CELLS = 512
CHIPS = 8
RING = 16
EARLY_STEPS = 6
PART = ROWS // 2
ROUNDS = ((1, 0), (1, 1), (2, 0), (2, 1), (3, 0), (3, 1), (4, 0), (4, 1), (0, 2), (5, 0), (5, 1), (1, 2), (2, 2))
ROUNDS += ((0, 3), (3, 2), (1, 3), (4, 2), (2, 3), (5, 2), (3, 3), (4, 3), (5, 3))


def kernel(
    owner_hbm,
    label_hbm,
    values_hbm,
    fields_hbm,
    green_hbm,
    parts,
    owner_ref,
    label_ref,
    values_ref,
    sent,
    sent_labels,
    got,
    got_labels,
    gathered,
    res,
    green,
    fields,
    acc_re,
    acc_im,
    load_sem,
    hand_sem,
    trace_sem,
    trace_recv,
    label_recv,
    green_send,
    green_recv,
    pair_send,
    pair_recv,
    own_sem,
    twin_send,
    twin_recv,
    res_send,
    res_recv,
    give_send,
    give_recv,
    sum_sem,
    from_left,
    from_right,
    across,
):
    slab = lax.axis_index("slab")
    src = lax.axis_index("src")
    z, core = slab // 2, slab % 2
    y, x, h = src // 8, (src // 2) % 4, src % 2
    ring = h * CHIPS + z

    loads = []
    for i, (a, b) in enumerate(
        (
            (owner_hbm, owner_ref),
            (label_hbm, label_ref),
            (values_hbm, values_ref),
            (green_hbm, green.at[slab]),
            (fields_hbm, fields),
        )
    ):
        loads.append(pltpu.make_async_copy(a, b, load_sem.at[i]))
        loads[-1].start()

    def at(dx, dy, hh):
        return (((y + dy + 4) % 4) * 4 + (x + dx + 4) % 4) * 2 + hh

    def along(d, to_core=core):
        to = (ring + d + RING) % RING
        return {"slab": (to % CHIPS) * 2 + to_core, "src": src - h + to // CHIPS}

    gap = jnp.where(h == 0, CHIPS - 1 - z, z)
    inward = 1 - 2 * h
    barrier = pltpu.get_barrier_semaphore()

    def greet(other):
        pl.semaphore_signal(barrier, inc=1, device_id=other, device_id_type=MESH)

    greet({"slab": z * 2 + 1 - core})

    @pl.when(z > 0)
    def _():
        greet(along(-1))

    @pl.when(z < CHIPS - 1)
    def _():
        greet(along(1))

    @pl.when(core == 1)
    def _():
        for dx, dy in ((1, 0), (-1, 0), (0, 1), (0, -1)):
            greet({"src": at(dx, dy, h)})

        @pl.when(gap == 0)
        def _():
            greet(along(inward, 0))

    greeted = 1 + (z > 0).astype(jnp.int32) + (z < CHIPS - 1).astype(jnp.int32)
    greeted += jnp.where(core == 1, 4, (gap == 0).astype(jnp.int32))

    def remote(src_ref, dst_ref, send_sem, recv_sem, to):
        return pltpu.make_async_remote_copy(
            src_ref=src_ref,
            dst_ref=dst_ref,
            send_sem=send_sem,
            recv_sem=recv_sem,
            device_id=to,
            device_id_type=MESH,
        )

    def arrived(ref, sem):
        pltpu.make_async_copy(ref, ref, sem).wait()

    partner = {"slab": z * 2 + 1 - core}
    hand_values = remote(sent.at[0], sent.at[0], hand_sem.at[0], hand_sem.at[1], partner)
    hand_labels = remote(
        sent_labels.at[0], sent_labels.at[0], hand_sem.at[2], hand_sem.at[3], partner
    )
    own_block = green.at[z * 2 + 1]
    own_copy = remote(green_hbm, own_block, own_sem.at[0], own_sem.at[1], partner)

    def place_traces():
        loads[0].wait()
        loads[1].wait()
        owners = owner_ref[...]
        labels = label_ref[...]
        hits = lax.broadcasted_iota(jnp.int32, (SLABS, ROWS), 0) == owners
        hits_f = hits.astype(jnp.float32)
        earlier = lax.broadcasted_iota(jnp.int32, (ROWS, ROWS), 0) < lax.broadcasted_iota(
            jnp.int32, (ROWS, ROWS), 1
        )
        counts = jnp.dot(
            hits_f.astype(jnp.bfloat16),
            earlier.astype(jnp.float32).astype(jnp.bfloat16),
            preferred_element_type=jnp.float32,
        )
        ranks = jnp.sum(counts * hits_f, axis=0, keepdims=True).astype(jnp.int32)
        slots = owners * CAP + ranks
        placing = (
            (lax.broadcasted_iota(jnp.int32, (SLABS * CAP, ROWS), 0) == slots)
            .astype(jnp.float32)
            .astype(jnp.bfloat16)
        )
        rank_hits = (
            (lax.broadcasted_iota(jnp.int32, (128, ROWS), 0) % CAP == ranks)
            .astype(jnp.float32)
            .astype(jnp.bfloat16)
        )
        high = (labels // 32).astype(jnp.float32)
        low = (labels % 32 + 1).astype(jnp.float32)
        codes = jnp.concatenate([hits_f * high, hits_f * low], axis=0).astype(jnp.bfloat16)
        placed_codes = lax.dot_general(
            codes, rank_hits, (((1,), (1,)), ((), ())), preferred_element_type=jnp.float32
        )
        label_rows = placed_codes[:SLABS] * 32.0 + placed_codes[SLABS:] - 1.0
        for k in range(SLABS):
            sent_labels[core, k] = label_rows[k : k + 1, :]
        loads[2].wait()
        placed = jnp.dot(placing, values_ref[...], preferred_element_type=jnp.float32)
        sent[core] = placed.astype(jnp.bfloat16).reshape(SLABS, CAP, 128)

    def green_copy(block, piece, d, source=None):
        ref = green.at[block * 2 + piece // 2, piece % 2]
        to = {"slab": slab + 2 * d}
        return remote(source or ref, ref, green_send, green_recv.at[block, piece], to)

    def pair_copy(block, piece):
        ref = green.at[block * 2 + piece // 2, piece % 2]
        return remote(ref, ref, pair_send, pair_recv.at[block], partner)

    def green_wait(block, piece):
        arrived(green.at[block * 2 + piece // 2, piece % 2], green_recv.at[block, piece])

    def green_start(piece):
        source = green_hbm.at[piece] if piece < 2 else None

        @pl.when(z < CHIPS - 1)
        def _():
            green_copy(z, piece, 1, source).start()

        @pl.when(z > 0)
        def _():
            green_copy(z, piece, -1, source).start()

    def green_step(step):
        for piece in range(4):

            @pl.when(z >= step)
            def _():
                green_wait(z - step, piece)

                @pl.when(z < CHIPS - 1)
                def _():
                    green_copy(z - step, piece, 1).start()

                pair_copy(z - step, piece).start()

            @pl.when(z + step < CHIPS)
            def _():
                green_wait(z + step, piece)

                @pl.when(z > 0)
                def _():
                    green_copy(z + step, piece, -1).start()

                pair_copy(z + step, piece).start()

    def trace_send(chip):
        to = {"slab": chip * 2 + core}
        owners_of = pl.ds(chip * 2, 2)
        remote(sent.at[:, owners_of], got.at[z], trace_sem.at[0], trace_recv.at[z], to).start()
        remote(
            sent_labels.at[:, owners_of], got_labels.at[z], trace_sem.at[1], label_recv.at[z], to
        ).start()

    def all_traces(i):
        arrived((got, got_labels)[i].at[pl.ds(0, CHIPS - 1)], trace_sem.at[i])

    def assemble(chip, first):
        low_lanes = lax.broadcasted_iota(jnp.int32, (1, 128), 1) < CAP
        rows_f = lax.broadcasted_iota(jnp.int32, (ROWS, 128), 0).astype(jnp.float32)
        for owner in range(2):
            row = jnp.where(low_lanes, got_labels[chip, 0, owner], got_labels[chip, 1, owner])
            picks = (rows_f == row).astype(jnp.float32).astype(jnp.bfloat16)
            term = jnp.dot(
                picks, got[chip, :, owner].reshape(128, 128), preferred_element_type=jnp.float32
            )
            gathered[owner] = term if first else gathered[owner] + term

    def chip_of(n):
        m = jnp.minimum(z, CHIPS - 1 - z)
        side = z + jnp.where(n % 2 == 1, -((n + 1) // 2), n // 2)
        rest = jnp.where(z < CHIPS // 2, n, CHIPS - 1 - n)
        return jnp.where(n <= 2 * m, side, rest)

    def trace_steps(first, last):
        for s in range(first, last + 1):

            @pl.when(z >= s)
            def _():
                if s > 1:
                    pl.semaphore_wait(from_left.at[s - 2], 1)

                @pl.when(z < CHIPS - 1)
                def _():
                    pl.semaphore_signal(
                        from_left.at[s - 1], inc=1, device_id=along(1), device_id_type=MESH
                    )

                trace_send(z - s)

            @pl.when(z + s < CHIPS)
            def _():
                if s > 1:
                    pl.semaphore_wait(from_right.at[s - 2], 1)

                @pl.when(z > 0)
                def _():
                    pl.semaphore_signal(
                        from_right.at[s - 1], inc=1, device_id=along(-1), device_id_type=MESH
                    )

                trace_send(z + s)

    def other_line():
        pl.semaphore_wait(across, 1)

        @pl.when(gap < CHIPS - 1)
        def _():
            pl.semaphore_signal(across, inc=1, device_id=along(-inward), device_id_type=MESH)

    def block_of(half, a, b, hh):
        return at(a, b, hh) if half == 0 else at(b, a, hh)

    def res_copy(half, a, b, hh, chunk, quarter, way, sem):
        first = half * ROWS + chunk * PART + max(quarter, 0) * (PART // 2)
        count = PART if quarter < 0 else PART // 2
        ref = res.at[block_of(half, a, b, hh), pl.ds(first, count), :]
        to = {"src": block_of(half, way[0], way[1], h)}
        remote(ref, ref, res_send, res_recv.at[sem], to).start()

    def give(turn, a, b):
        ref = res.at[at(a, b, (h, 1 - h)[turn // 2]), pl.ds(turn % 2 * PART, PART), :]
        remote(ref, ref, give_send, give_recv.at[turn], partner).start()

    RIGHT, LEFT, UP, DOWN = (1, 0), (-1, 0), (0, 1), (0, -1)

    def res_round(step, turn):
        hh, chunk = (h, 1 - h)[turn // 2], turn % 2
        for half in range(2):

            def sem(number):
                return (turn * 5 + number - 1) * 2 + half

            if step > 0:
                ref = (
                    res.at[0, pl.ds(0, ROWS), :],
                    res.at[0, pl.ds(0, PART), :],
                    res.at[pl.ds(0, 3), pl.ds(0, ROWS), :],
                    res.at[0, pl.ds(0, ROWS), :],
                    res.at[0],
                )[step - 1]
                arrived(ref, res_recv.at[sem(step)])
            if step == 0:
                res_copy(half, 0, 0, hh, chunk, -1, RIGHT, sem(1))
                res_copy(half, 0, 0, hh, chunk, -1, LEFT, sem(1))
            elif step == 1:
                res_copy(half, -1, 0, hh, chunk, 0, RIGHT, sem(2))
                res_copy(half, 1, 0, hh, chunk, 1, LEFT, sem(2))
            elif step == 3:
                for a in (0, -1, 1):
                    res_copy(half, a, -1, hh, chunk, 0, UP, sem(5))
                    res_copy(half, a, 1, hh, chunk, 1, DOWN, sem(5))
            elif step == 4:
                res_copy(half, 2, -1, hh, chunk, 0, UP, sem(5))
                res_copy(half, 2, 1, hh, chunk, 1, DOWN, sem(5))
        if step < 3:
            for half in range(2):
                number = (turn * 5 + (3 if step < 2 else 4) - 1) * 2 + half
                for a in ((0,), (-1, 1), (2,))[step]:
                    res_copy(half, a, 0, hh, chunk, -1, UP, number)
                    res_copy(half, a, 0, hh, chunk, -1, DOWN, number)
        for a, b in (
            ((0, 0),),
            ((-1, 0), (1, 0)),
            ((2, 0),),
            ((0, -1), (0, 1), (-1, -1), (-1, 1), (1, -1), (1, 1)),
            ((2, -1), (2, 1)),
            ((0, 2), (-1, 2), (1, 2), (2, 2)),
        )[step]:
            give(turn, a, b)

    @pl.when(core == 0)
    def _():
        pl.semaphore_wait(barrier, greeted)
        for piece in range(2):
            green_start(piece)

    @pl.when(core == 1)
    def _():
        pl.semaphore_wait(barrier, greeted)
        own_copy.start()

    place_traces()
    loads[3].wait()

    @pl.when(core == 0)
    def _():
        hand_labels.start()
        hand_values.start()
        arrived(own_block, own_sem.at[1])
        for piece in range(2, 4):
            green_start(piece)
        for piece in range(2):
            pair_copy(z, piece).start()
        for step in range(1, EARLY_STEPS + 1):
            if step == 2:

                @pl.when(gap == 0)
                def _():
                    pl.semaphore_wait(across, 1)
                    pl.semaphore_signal(
                        across, inc=1, device_id=along(inward, 1), device_id_type=MESH
                    )

            green_step(step)
        for turn in range(4):
            arrived(res.at[pl.ds(0, SRCS // 8)], give_recv.at[turn])

    @pl.when(core == 1)
    def _():
        arrived(sent_labels.at[0], hand_sem.at[3])
        arrived(sent.at[0], hand_sem.at[1])
        trace_steps(1, CHIPS - 1)
        for i in range(2):
            got[z, i] = sent[i, pl.ds(z * 2, 2)]
            got_labels[z, i] = sent_labels[i, pl.ds(z * 2, 2)]

        @pl.when(gap == 0)
        def _():
            pl.semaphore_signal(across, inc=1, device_id=partner, device_id_type=MESH)

        @pl.when(gap <= 4)
        def _():
            other_line()

        assemble(z, True)

        def next_chip(n, carry):
            chip = chip_of(n)
            arrived(got_labels.at[chip], label_recv.at[chip])
            arrived(got.at[chip], trace_recv.at[chip])
            assemble(chip, False)
            return carry

        lax.fori_loop(1, CHIPS, next_chip, 0)
        for owner in range(2):
            res[src, pl.ds(owner * ROWS, ROWS), :] = gathered[owner].astype(jnp.bfloat16)

        res_round(0, 0)
        res_round(0, 1)

        @pl.when(gap > 4)
        def _():
            other_line()

        twin = at(0, 0, 1 - h)
        for chunk in range(2):
            for half in range(2):
                ref = res.at[src, pl.ds(half * ROWS + chunk * PART, PART), :]
                remote(ref, ref, twin_send, twin_recv.at[chunk], {"src": twin}).start()
        for step, turn in ROUNDS:
            if step == 0:
                arrived(res.at[0, pl.ds(0, ROWS), :], twin_recv.at[turn - 2])
            res_round(step, turn)
        arrived(res.at[0], twin_send)

    acc_re[...] = jnp.zeros_like(acc_re)
    acc_im[...] = jnp.zeros_like(acc_im)
    loads[4].wait()

    def multiply(n, carry):
        block = chip_of(n)
        far = jnp.abs(block - z)
        before = jnp.abs(chip_of(jnp.maximum(n - 1, 0)) - z)

        @pl.when((core == 0) & (far > EARLY_STEPS) & (far > before))
        def _():
            green_step(far)

        @pl.when((core == 1) & (far == 0))
        def _():
            arrived(green.at[0], pair_recv.at[block])

        @pl.when((core == 1) & (far > 0))
        def _():
            arrived(green.at[pl.ds(0, 2)], pair_recv.at[block])

        for i in range(2):
            index = block * 2 + i
            rows = pl.ds(pl.multiple_of(core * ROWS, ROWS), ROWS)
            left = jnp.concatenate([res[2 * index, rows, :], res[2 * index + 1, rows, :]], axis=1)
            g_re = green[index, 0]
            g_im = green[index, 1]
            right_re = jnp.concatenate([g_re[:CAP], g_im[:CAP], g_re[CAP:], g_im[CAP:]], axis=0)
            right_im = jnp.concatenate([g_im[:CAP], -g_re[:CAP], g_im[CAP:], -g_re[CAP:]], axis=0)
            acc_re[...] += jnp.dot(left, right_re, preferred_element_type=jnp.float32)
            acc_im[...] += jnp.dot(left, right_im, preferred_element_type=jnp.float32)
        return carry

    lax.fori_loop(0, CHIPS, multiply, 0)
    partial = jnp.sum(
        fields[0].astype(jnp.float32) * acc_re[...] - fields[1].astype(jnp.float32) * acc_im[...],
        axis=0,
        keepdims=True,
    )
    parts[slab] = partial
    for d in range(1, SLABS):
        to = {"slab": (slab + d) % SLABS}
        remote(parts.at[slab], parts.at[slab], sum_sem.at[0], sum_sem.at[1], to).start()

    end = (z == 0) | (z == CHIPS - 1)

    @pl.when(core == 0)
    def _():
        hand_values.wait_send()
        hand_labels.wait_send()
        arrived(green.at[pl.ds(0, SLABS - 1)], pair_send)

        @pl.when(end)
        def _():
            arrived(res.at[pl.ds(0, 2)], green_send)

        @pl.when(jnp.logical_not(end))
        def _():
            arrived(res.at[pl.ds(0, 2 * CHIPS + 2)], green_send)

    @pl.when(core == 1)
    def _():
        own_copy.wait_send()
        all_traces(0)
        all_traces(1)
        arrived(res.at[pl.ds(0, SRCS - 2)], res_send)
        arrived(res.at[pl.ds(0, SRCS // 2)], give_send)

    arrived(parts.at[pl.ds(0, SLABS - 1)], sum_sem.at[1])
    arrived(parts.at[pl.ds(0, SLABS - 1)], sum_sem.at[0])


def total(parts_ref, out_ref):
    out_ref[...] = jnp.sum(parts_ref[...], axis=0)


def on_device(trace_values, trace_owner, trace_source, source_fields, green_fields):
    dma = pltpu.SemaphoreType.DMA
    vmem = pl.BlockSpec(memory_space=pltpu.VMEM)
    parts = pl.pallas_call(
        kernel,
        out_shape=jax.ShapeDtypeStruct((SLABS, 1, CELLS), jnp.float32),
        in_specs=[pl.BlockSpec(memory_space=pltpu.HBM)] * 5,
        out_specs=vmem,
        scratch_shapes=[
            pltpu.VMEM((1, ROWS), jnp.int32),
            pltpu.VMEM((1, ROWS), jnp.int32),
            pltpu.VMEM((ROWS, 128), jnp.bfloat16),
            pltpu.VMEM((2, SLABS, CAP, 128), jnp.bfloat16),
            pltpu.VMEM((2, SLABS, 1, 128), jnp.float32),
            pltpu.VMEM((CHIPS, 2, 2, CAP, 128), jnp.bfloat16),
            pltpu.VMEM((CHIPS, 2, 2, 1, 128), jnp.float32),
            pltpu.VMEM((2, ROWS, 128), jnp.float32),
            pltpu.VMEM((SRCS, 2 * ROWS, 128), jnp.bfloat16),
            pltpu.VMEM((SLABS, 2, 128, CELLS), jnp.bfloat16),
            pltpu.VMEM((2, ROWS, CELLS), jnp.bfloat16),
            pltpu.VMEM((ROWS, CELLS), jnp.float32),
            pltpu.VMEM((ROWS, CELLS), jnp.float32),
            dma((5,)),
            dma((4,)),
            dma((2,)),
            dma((CHIPS,)),
            dma((CHIPS,)),
            dma,
            dma((CHIPS, 4)),
            dma,
            dma((CHIPS,)),
            dma((2,)),
            dma,
            dma((2,)),
            dma,
            dma((40,)),
            dma,
            dma((4,)),
            dma((2,)),
            pltpu.SemaphoreType.REGULAR((CHIPS - 1,)),
            pltpu.SemaphoreType.REGULAR((CHIPS - 1,)),
            pltpu.SemaphoreType.REGULAR,
        ],
        compiler_params=pltpu.CompilerParams(
            collective_id=0, has_side_effects=True, vmem_limit_bytes=60 * 1024 * 1024
        ),
    )(
        trace_owner.reshape(1, ROWS),
        trace_source.reshape(1, ROWS),
        trace_values[0],
        source_fields,
        green_fields,
    )
    out = pl.pallas_call(
        total,
        out_shape=jax.ShapeDtypeStruct((1, CELLS), jnp.float32),
        in_specs=[vmem],
        out_specs=vmem,
    )(parts)
    return out.reshape(CELLS)


def solution(mesh):
    in_specs = (
        P("src", "slab", None),
        P("src", "slab", None),
        P("src", "slab"),
        P(None, "slab", "src"),
        P(None, "slab", "src"),
    )
    return jax.shard_map(
        on_device, mesh=mesh, in_specs=in_specs, out_specs=P("src"), check_vma=False
    )
```

```python
import jax
import jax.numpy as jnp
from jax import lax
from jax.experimental import pallas as pl
from jax.experimental.pallas import tpu as pltpu
from jax.sharding import PartitionSpec as P

MESH = pl.DeviceIdType.MESH
SLABS = 16
SRCS = 32
CAP = 64
ROWS = 512
CELLS = 512
CHIPS = 8
RING = 16
EARLY_STEPS = 6
PART = ROWS // 2
ROUNDS = ((1, 0), (1, 1), (2, 0), (2, 1), (3, 0), (3, 1), (4, 0), (4, 1), (0, 2), (5, 0), (5, 1), (1, 2), (2, 2))
ROUNDS += ((0, 3), (3, 2), (1, 3), (4, 2), (2, 3), (5, 2), (3, 3), (4, 3), (5, 3))


def kernel(
    owner_hbm,
    label_hbm,
    values_hbm,
    fields_hbm,
    green_hbm,
    parts,
    owner_ref,
    label_ref,
    values_ref,
    sent,
    sent_labels,
    got,
    got_labels,
    gathered,
    res,
    green,
    fields,
    acc_re,
    acc_im,
    load_sem,
    hand_sem,
    trace_sem,
    trace_recv,
    label_recv,
    green_send,
    green_recv,
    pair_send,
    pair_recv,
    own_sem,
    twin_send,
    twin_recv,
    res_send,
    res_recv,
    give_send,
    give_recv,
    sum_sem,
    from_left,
    from_right,
    across,
):
    slab = lax.axis_index("slab")
    src = lax.axis_index("src")
    z, core = slab // 2, slab % 2
    y, x, h = src // 8, (src // 2) % 4, src % 2
    ring = h * CHIPS + z

    loads = []
    for i, (a, b) in enumerate(
        (
            (owner_hbm, owner_ref),
            (label_hbm, label_ref),
            (values_hbm, values_ref),
            (green_hbm, green.at[slab]),
            (fields_hbm, fields),
        )
    ):
        loads.append(pltpu.make_async_copy(a, b, load_sem.at[i]))
        loads[-1].start()

    def at(dx, dy, hh):
        return (((y + dy + 4) % 4) * 4 + (x + dx + 4) % 4) * 2 + hh

    def along(d, to_core=core):
        to = (ring + d + RING) % RING
        return {"slab": (to % CHIPS) * 2 + to_core, "src": src - h + to // CHIPS}

    gap = jnp.where(h == 0, CHIPS - 1 - z, z)
    inward = 1 - 2 * h
    barrier = pltpu.get_barrier_semaphore()

    def greet(other):
        pl.semaphore_signal(barrier, inc=1, device_id=other, device_id_type=MESH)

    greet({"slab": z * 2 + 1 - core})

    @pl.when(z > 0)
    def _():
        greet(along(-1))

    @pl.when(z < CHIPS - 1)
    def _():
        greet(along(1))

    @pl.when(core == 1)
    def _():
        for dx, dy in ((1, 0), (-1, 0), (0, 1), (0, -1)):
            greet({"src": at(dx, dy, h)})

        @pl.when(gap == 0)
        def _():
            greet(along(inward, 0))

    greeted = 1 + (z > 0).astype(jnp.int32) + (z < CHIPS - 1).astype(jnp.int32)
    greeted += jnp.where(core == 1, 4, (gap == 0).astype(jnp.int32))

    def remote(src_ref, dst_ref, send_sem, recv_sem, to):
        return pltpu.make_async_remote_copy(
            src_ref=src_ref,
            dst_ref=dst_ref,
            send_sem=send_sem,
            recv_sem=recv_sem,
            device_id=to,
            device_id_type=MESH,
        )

    def arrived(ref, sem):
        pltpu.make_async_copy(ref, ref, sem).wait()

    partner = {"slab": z * 2 + 1 - core}
    hand_values = remote(sent.at[0], sent.at[0], hand_sem.at[0], hand_sem.at[1], partner)
    hand_labels = remote(
        sent_labels.at[0], sent_labels.at[0], hand_sem.at[2], hand_sem.at[3], partner
    )
    own_block = green.at[z * 2 + 1]
    own_copy = remote(green_hbm, own_block, own_sem.at[0], own_sem.at[1], partner)

    def place_traces():
        loads[0].wait()
        loads[1].wait()
        owners = owner_ref[...]
        labels = label_ref[...]
        hits = lax.broadcasted_iota(jnp.int32, (SLABS, ROWS), 0) == owners
        hits_f = hits.astype(jnp.float32)
        earlier = lax.broadcasted_iota(jnp.int32, (ROWS, ROWS), 0) < lax.broadcasted_iota(
            jnp.int32, (ROWS, ROWS), 1
        )
        counts = jnp.dot(
            hits_f.astype(jnp.bfloat16),
            earlier.astype(jnp.float32).astype(jnp.bfloat16),
            preferred_element_type=jnp.float32,
        )
        ranks = jnp.sum(counts * hits_f, axis=0, keepdims=True).astype(jnp.int32)
        slots = owners * CAP + ranks
        placing = (
            (lax.broadcasted_iota(jnp.int32, (SLABS * CAP, ROWS), 0) == slots)
            .astype(jnp.float32)
            .astype(jnp.bfloat16)
        )
        rank_hits = (
            (lax.broadcasted_iota(jnp.int32, (128, ROWS), 0) % CAP == ranks)
            .astype(jnp.float32)
            .astype(jnp.bfloat16)
        )
        high = (labels // 32).astype(jnp.float32)
        low = (labels % 32 + 1).astype(jnp.float32)
        codes = jnp.concatenate([hits_f * high, hits_f * low], axis=0).astype(jnp.bfloat16)
        placed_codes = lax.dot_general(
            codes, rank_hits, (((1,), (1,)), ((), ())), preferred_element_type=jnp.float32
        )
        label_rows = placed_codes[:SLABS] * 32.0 + placed_codes[SLABS:] - 1.0
        for k in range(SLABS):
            sent_labels[core, k] = label_rows[k : k + 1, :]
        loads[2].wait()
        placed = jnp.dot(placing, values_ref[...], preferred_element_type=jnp.float32)
        sent[core] = placed.astype(jnp.bfloat16).reshape(SLABS, CAP, 128)

    def green_copy(block, piece, d, source=None):
        ref = green.at[block * 2 + piece // 2, piece % 2]
        to = {"slab": slab + 2 * d}
        return remote(source or ref, ref, green_send, green_recv.at[block, piece], to)

    def pair_copy(block, piece):
        ref = green.at[block * 2 + piece // 2, piece % 2]
        return remote(ref, ref, pair_send, pair_recv.at[block], partner)

    def green_wait(block, piece):
        arrived(green.at[block * 2 + piece // 2, piece % 2], green_recv.at[block, piece])

    def green_start(piece):
        source = green_hbm.at[piece] if piece < 2 else None

        @pl.when(z < CHIPS - 1)
        def _():
            green_copy(z, piece, 1, source).start()

        @pl.when(z > 0)
        def _():
            green_copy(z, piece, -1, source).start()

    def green_step(step):
        for piece in range(4):

            @pl.when(z >= step)
            def _():
                green_wait(z - step, piece)

                @pl.when(z < CHIPS - 1)
                def _():
                    green_copy(z - step, piece, 1).start()

                pair_copy(z - step, piece).start()

            @pl.when(z + step < CHIPS)
            def _():
                green_wait(z + step, piece)

                @pl.when(z > 0)
                def _():
                    green_copy(z + step, piece, -1).start()

                pair_copy(z + step, piece).start()

    def trace_send(chip):
        to = {"slab": chip * 2 + core}
        owners_of = pl.ds(chip * 2, 2)
        remote(sent.at[:, owners_of], got.at[z], trace_sem.at[0], trace_recv.at[z], to).start()
        remote(
            sent_labels.at[:, owners_of], got_labels.at[z], trace_sem.at[1], label_recv.at[z], to
        ).start()

    def all_traces(i):
        arrived((got, got_labels)[i].at[pl.ds(0, CHIPS - 1)], trace_sem.at[i])

    def assemble(chip, first):
        low_lanes = lax.broadcasted_iota(jnp.int32, (1, 128), 1) < CAP
        rows_f = lax.broadcasted_iota(jnp.int32, (ROWS, 128), 0).astype(jnp.float32)
        for owner in range(2):
            row = jnp.where(low_lanes, got_labels[chip, 0, owner], got_labels[chip, 1, owner])
            picks = (rows_f == row).astype(jnp.float32).astype(jnp.bfloat16)
            term = jnp.dot(
                picks, got[chip, :, owner].reshape(128, 128), preferred_element_type=jnp.float32
            )
            gathered[owner] = term if first else gathered[owner] + term

    def chip_of(n):
        m = jnp.minimum(z, CHIPS - 1 - z)
        side = z + jnp.where(n % 2 == 1, -((n + 1) // 2), n // 2)
        rest = jnp.where(z < CHIPS // 2, n, CHIPS - 1 - n)
        return jnp.where(n <= 2 * m, side, rest)

    def trace_steps(first, last):
        for s in range(first, last + 1):

            @pl.when(z >= s)
            def _():
                if s > 1:
                    pl.semaphore_wait(from_left.at[s - 2], 1)

                @pl.when(z < CHIPS - 1)
                def _():
                    pl.semaphore_signal(
                        from_left.at[s - 1], inc=1, device_id=along(1), device_id_type=MESH
                    )

                trace_send(z - s)

            @pl.when(z + s < CHIPS)
            def _():
                if s > 1:
                    pl.semaphore_wait(from_right.at[s - 2], 1)

                @pl.when(z > 0)
                def _():
                    pl.semaphore_signal(
                        from_right.at[s - 1], inc=1, device_id=along(-1), device_id_type=MESH
                    )

                trace_send(z + s)

    def other_line():
        pl.semaphore_wait(across, 1)

        @pl.when(gap < CHIPS - 1)
        def _():
            pl.semaphore_signal(across, inc=1, device_id=along(-inward), device_id_type=MESH)

    def block_of(half, a, b, hh):
        return at(a, b, hh) if half == 0 else at(b, a, hh)

    def res_copy(half, a, b, hh, chunk, quarter, way, sem):
        first = half * ROWS + chunk * PART + max(quarter, 0) * (PART // 2)
        count = PART if quarter < 0 else PART // 2
        ref = res.at[block_of(half, a, b, hh), pl.ds(first, count), :]
        to = {"src": block_of(half, way[0], way[1], h)}
        remote(ref, ref, res_send, res_recv.at[sem], to).start()

    def give(turn, a, b):
        ref = res.at[at(a, b, (h, 1 - h)[turn // 2]), pl.ds(turn % 2 * PART, PART), :]
        remote(ref, ref, give_send, give_recv.at[turn], partner).start()

    RIGHT, LEFT, UP, DOWN = (1, 0), (-1, 0), (0, 1), (0, -1)

    def res_round(step, turn):
        hh, chunk = (h, 1 - h)[turn // 2], turn % 2
        for half in range(2):

            def sem(number):
                return (turn * 5 + number - 1) * 2 + half

            if step > 0:
                ref = (
                    res.at[0, pl.ds(0, ROWS), :],
                    res.at[0, pl.ds(0, PART), :],
                    res.at[pl.ds(0, 3), pl.ds(0, ROWS), :],
                    res.at[0, pl.ds(0, ROWS), :],
                    res.at[0],
                )[step - 1]
                arrived(ref, res_recv.at[sem(step)])
            if step == 0:
                res_copy(half, 0, 0, hh, chunk, -1, RIGHT, sem(1))
                res_copy(half, 0, 0, hh, chunk, -1, LEFT, sem(1))
            elif step == 1:
                res_copy(half, -1, 0, hh, chunk, 0, RIGHT, sem(2))
                res_copy(half, 1, 0, hh, chunk, 1, LEFT, sem(2))
            elif step == 3:
                for a in (0, -1, 1):
                    res_copy(half, a, -1, hh, chunk, 0, UP, sem(5))
                    res_copy(half, a, 1, hh, chunk, 1, DOWN, sem(5))
            elif step == 4:
                res_copy(half, 2, -1, hh, chunk, 0, UP, sem(5))
                res_copy(half, 2, 1, hh, chunk, 1, DOWN, sem(5))
        if step < 3:
            for half in range(2):
                number = (turn * 5 + (3 if step < 2 else 4) - 1) * 2 + half
                for a in ((0,), (-1, 1), (2,))[step]:
                    res_copy(half, a, 0, hh, chunk, -1, UP, number)
                    res_copy(half, a, 0, hh, chunk, -1, DOWN, number)
        for a, b in (
            ((0, 0),),
            ((-1, 0), (1, 0)),
            ((2, 0),),
            ((0, -1), (0, 1), (-1, -1), (-1, 1), (1, -1), (1, 1)),
            ((2, -1), (2, 1)),
            ((0, 2), (-1, 2), (1, 2), (2, 2)),
        )[step]:
            give(turn, a, b)

    @pl.when(core == 0)
    def _():
        pl.semaphore_wait(barrier, greeted)
        for piece in range(2):
            green_start(piece)

    @pl.when(core == 1)
    def _():
        pl.semaphore_wait(barrier, greeted)
        own_copy.start()

    place_traces()
    loads[3].wait()

    @pl.when(core == 0)
    def _():
        hand_labels.start()
        hand_values.start()
        arrived(own_block, own_sem.at[1])
        for piece in range(2, 4):
            green_start(piece)
        for piece in range(2):
            pair_copy(z, piece).start()
        for step in range(1, EARLY_STEPS + 1):
            if step == 2:

                @pl.when(gap == 0)
                def _():
                    pl.semaphore_wait(across, 1)
                    pl.semaphore_signal(
                        across, inc=1, device_id=along(inward, 1), device_id_type=MESH
                    )

            green_step(step)
        for turn in range(4):
            arrived(res.at[pl.ds(0, SRCS // 8)], give_recv.at[turn])

    @pl.when(core == 1)
    def _():
        arrived(sent_labels.at[0], hand_sem.at[3])
        arrived(sent.at[0], hand_sem.at[1])
        trace_steps(1, CHIPS - 1)
        for i in range(2):
            got[z, i] = sent[i, pl.ds(z * 2, 2)]
            got_labels[z, i] = sent_labels[i, pl.ds(z * 2, 2)]

        @pl.when(gap == 0)
        def _():
            pl.semaphore_signal(across, inc=1, device_id=partner, device_id_type=MESH)

        @pl.when(gap <= 4)
        def _():
            other_line()

        assemble(z, True)

        def next_chip(n, carry):
            chip = chip_of(n)
            arrived(got_labels.at[chip], label_recv.at[chip])
            arrived(got.at[chip], trace_recv.at[chip])
            assemble(chip, False)
            return carry

        lax.fori_loop(1, CHIPS, next_chip, 0)
        for owner in range(2):
            res[src, pl.ds(owner * ROWS, ROWS), :] = gathered[owner].astype(jnp.bfloat16)

        res_round(0, 0)
        res_round(0, 1)

        @pl.when(gap > 4)
        def _():
            other_line()

        twin = at(0, 0, 1 - h)
        for chunk in range(2):
            for half in range(2):
                ref = res.at[src, pl.ds(half * ROWS + chunk * PART, PART), :]
                remote(ref, ref, twin_send, twin_recv.at[chunk], {"src": twin}).start()
        for step, turn in ROUNDS:
            if step == 0:
                arrived(res.at[0, pl.ds(0, ROWS), :], twin_recv.at[turn - 2])
            res_round(step, turn)
        arrived(res.at[0], twin_send)

    acc_re[...] = jnp.zeros_like(acc_re)
    acc_im[...] = jnp.zeros_like(acc_im)
    loads[4].wait()

    def multiply(n, carry):
        block = chip_of(n)
        far = jnp.abs(block - z)
        before = jnp.abs(chip_of(jnp.maximum(n - 1, 0)) - z)

        @pl.when((core == 0) & (far > EARLY_STEPS) & (far > before))
        def _():
            green_step(far)

        @pl.when((core == 1) & (far == 0))
        def _():
            arrived(green.at[0], pair_recv.at[block])

        @pl.when((core == 1) & (far > 0))
        def _():
            arrived(green.at[pl.ds(0, 2)], pair_recv.at[block])

        rows = pl.ds(pl.multiple_of(core * ROWS, ROWS), ROWS)
        left = jnp.concatenate([res[4 * block + i, rows, :] for i in range(4)], axis=1)
        right_re, right_im = [], []
        for i in range(4):
            half = pl.ds(i % 2 * CAP, CAP)
            g_re, g_im = (green[block * 2 + i // 2, c, half, :] for c in range(2))
            right_re += [g_re, g_im]
            right_im += [g_im, -g_re]
        right_re, right_im = (jnp.concatenate(r, axis=0) for r in (right_re, right_im))
        acc_re[...] += jnp.dot(left, right_re, preferred_element_type=jnp.float32)
        acc_im[...] += jnp.dot(left, right_im, preferred_element_type=jnp.float32)
        return carry

    lax.fori_loop(0, CHIPS, multiply, 0)
    partial = jnp.sum(
        fields[0].astype(jnp.float32) * acc_re[...] - fields[1].astype(jnp.float32) * acc_im[...],
        axis=0,
        keepdims=True,
    )
    parts[slab] = partial
    for d in range(1, SLABS):
        to = {"slab": (slab + d) % SLABS}
        remote(parts.at[slab], parts.at[slab], sum_sem.at[0], sum_sem.at[1], to).start()

    end = (z == 0) | (z == CHIPS - 1)

    @pl.when(core == 0)
    def _():
        hand_values.wait_send()
        hand_labels.wait_send()
        arrived(green.at[pl.ds(0, SLABS - 1)], pair_send)

        @pl.when(end)
        def _():
            arrived(res.at[pl.ds(0, 2)], green_send)

        @pl.when(jnp.logical_not(end))
        def _():
            arrived(res.at[pl.ds(0, 2 * CHIPS + 2)], green_send)

    @pl.when(core == 1)
    def _():
        own_copy.wait_send()
        all_traces(0)
        all_traces(1)
        arrived(res.at[pl.ds(0, SRCS - 2)], res_send)
        arrived(res.at[pl.ds(0, SRCS // 2)], give_send)

    arrived(parts.at[pl.ds(0, SLABS - 1)], sum_sem.at[1])
    arrived(parts.at[pl.ds(0, SLABS - 1)], sum_sem.at[0])


def total(parts_ref, out_ref):
    out_ref[...] = jnp.sum(parts_ref[...], axis=0)


def on_device(trace_values, trace_owner, trace_source, source_fields, green_fields):
    dma = pltpu.SemaphoreType.DMA
    vmem = pl.BlockSpec(memory_space=pltpu.VMEM)
    parts = pl.pallas_call(
        kernel,
        out_shape=jax.ShapeDtypeStruct((SLABS, 1, CELLS), jnp.float32),
        in_specs=[pl.BlockSpec(memory_space=pltpu.HBM)] * 5,
        out_specs=vmem,
        scratch_shapes=[
            pltpu.VMEM((1, ROWS), jnp.int32),
            pltpu.VMEM((1, ROWS), jnp.int32),
            pltpu.VMEM((ROWS, 128), jnp.bfloat16),
            pltpu.VMEM((2, SLABS, CAP, 128), jnp.bfloat16),
            pltpu.VMEM((2, SLABS, 1, 128), jnp.float32),
            pltpu.VMEM((CHIPS, 2, 2, CAP, 128), jnp.bfloat16),
            pltpu.VMEM((CHIPS, 2, 2, 1, 128), jnp.float32),
            pltpu.VMEM((2, ROWS, 128), jnp.float32),
            pltpu.VMEM((SRCS, 2 * ROWS, 128), jnp.bfloat16),
            pltpu.VMEM((SLABS, 2, 128, CELLS), jnp.bfloat16),
            pltpu.VMEM((2, ROWS, CELLS), jnp.bfloat16),
            pltpu.VMEM((ROWS, CELLS), jnp.float32),
            pltpu.VMEM((ROWS, CELLS), jnp.float32),
            dma((5,)),
            dma((4,)),
            dma((2,)),
            dma((CHIPS,)),
            dma((CHIPS,)),
            dma,
            dma((CHIPS, 4)),
            dma,
            dma((CHIPS,)),
            dma((2,)),
            dma,
            dma((2,)),
            dma,
            dma((40,)),
            dma,
            dma((4,)),
            dma((2,)),
            pltpu.SemaphoreType.REGULAR((CHIPS - 1,)),
            pltpu.SemaphoreType.REGULAR((CHIPS - 1,)),
            pltpu.SemaphoreType.REGULAR,
        ],
        compiler_params=pltpu.CompilerParams(
            collective_id=0, has_side_effects=True, vmem_limit_bytes=60 * 1024 * 1024
        ),
    )(
        trace_owner.reshape(1, ROWS),
        trace_source.reshape(1, ROWS),
        trace_values[0],
        source_fields,
        green_fields,
    )
    out = pl.pallas_call(
        total,
        out_shape=jax.ShapeDtypeStruct((1, CELLS), jnp.float32),
        in_specs=[vmem],
        out_specs=vmem,
    )(parts)
    return out.reshape(CELLS)


def solution(mesh):
    in_specs = (
        P("src", "slab", None),
        P("src", "slab", None),
        P("src", "slab"),
        P(None, "slab", "src"),
        P(None, "slab", "src"),
    )
    return jax.shard_map(
        on_device, mesh=mesh, in_specs=in_specs, out_specs=P("src"), check_vma=False
    )
```

```python
import jax
import jax.numpy as jnp
from jax import lax
from jax.experimental import pallas as pl
from jax.experimental.pallas import tpu as pltpu
from jax.sharding import PartitionSpec as P

MESH = pl.DeviceIdType.MESH
SLABS = 16
SRCS = 32
CAP = 64
ROWS = 512
CELLS = 512
CHIPS = 8
RING = 16
EARLY_STEPS = 6
PART = ROWS // 2
ROUNDS = ((1, 0), (1, 1), (2, 0), (2, 1), (3, 0), (3, 1), (4, 0), (4, 1), (0, 2), (5, 0), (5, 1), (1, 2), (2, 2))
ROUNDS += ((0, 3), (3, 2), (1, 3), (4, 2), (2, 3), (5, 2), (3, 3), (4, 3), (5, 3))


def kernel(
    owner_hbm,
    label_hbm,
    values_hbm,
    fields_hbm,
    green_hbm,
    parts,
    owner_ref,
    label_ref,
    values_ref,
    sent,
    sent_labels,
    got,
    got_labels,
    gathered,
    res,
    green,
    fields,
    acc_re,
    acc_im,
    load_sem,
    hand_sem,
    trace_sem,
    trace_recv,
    label_recv,
    green_send,
    green_recv,
    pair_send,
    pair_recv,
    own_sem,
    twin_send,
    twin_recv,
    res_send,
    res_recv,
    give_send,
    give_recv,
    sum_sem,
    from_left,
    from_right,
    across,
):
    slab = lax.axis_index("slab")
    src = lax.axis_index("src")
    z, core = slab // 2, slab % 2
    y, x, h = src // 8, (src // 2) % 4, src % 2
    ring = h * CHIPS + z

    loads = []
    for i, (a, b) in enumerate(
        (
            (owner_hbm, owner_ref),
            (label_hbm, label_ref),
            (values_hbm, values_ref),
            (green_hbm, green.at[slab]),
            (fields_hbm, fields),
        )
    ):
        loads.append(pltpu.make_async_copy(a, b, load_sem.at[i]))
        loads[-1].start()

    def at(dx, dy, hh):
        return (((y + dy + 4) % 4) * 4 + (x + dx + 4) % 4) * 2 + hh

    def along(d, to_core=core):
        to = (ring + d + RING) % RING
        return {"slab": (to % CHIPS) * 2 + to_core, "src": src - h + to // CHIPS}

    gap = jnp.where(h == 0, CHIPS - 1 - z, z)
    inward = 1 - 2 * h
    barrier = pltpu.get_barrier_semaphore()

    def greet(other):
        pl.semaphore_signal(barrier, inc=1, device_id=other, device_id_type=MESH)

    greet({"slab": z * 2 + 1 - core})

    @pl.when(z > 0)
    def _():
        greet(along(-1))

    @pl.when(z < CHIPS - 1)
    def _():
        greet(along(1))

    @pl.when(core == 1)
    def _():
        for dx, dy in ((1, 0), (-1, 0), (0, 1), (0, -1)):
            greet({"src": at(dx, dy, h)})

        @pl.when(gap == 0)
        def _():
            greet(along(inward, 0))

    greeted = 1 + (z > 0).astype(jnp.int32) + (z < CHIPS - 1).astype(jnp.int32)
    greeted += jnp.where(core == 1, 4, (gap == 0).astype(jnp.int32))

    def remote(src_ref, dst_ref, send_sem, recv_sem, to):
        return pltpu.make_async_remote_copy(
            src_ref=src_ref,
            dst_ref=dst_ref,
            send_sem=send_sem,
            recv_sem=recv_sem,
            device_id=to,
            device_id_type=MESH,
        )

    def arrived(ref, sem):
        pltpu.make_async_copy(ref, ref, sem).wait()

    partner = {"slab": z * 2 + 1 - core}
    hand_values = remote(sent.at[0], sent.at[0], hand_sem.at[0], hand_sem.at[1], partner)
    hand_labels = remote(
        sent_labels.at[0], sent_labels.at[0], hand_sem.at[2], hand_sem.at[3], partner
    )
    own_block = green.at[z * 2 + 1]
    own_copy = remote(green_hbm, own_block, own_sem.at[0], own_sem.at[1], partner)

    def place_traces():
        loads[0].wait()
        loads[1].wait()
        owners = owner_ref[...]
        labels = label_ref[...]
        hits = lax.broadcasted_iota(jnp.int32, (SLABS, ROWS), 0) == owners
        hits_f = hits.astype(jnp.float32)
        earlier = lax.broadcasted_iota(jnp.int32, (ROWS, ROWS), 0) < lax.broadcasted_iota(
            jnp.int32, (ROWS, ROWS), 1
        )
        counts = jnp.dot(
            hits_f.astype(jnp.bfloat16),
            earlier.astype(jnp.float32).astype(jnp.bfloat16),
            preferred_element_type=jnp.float32,
        )
        ranks = jnp.sum(counts * hits_f, axis=0, keepdims=True).astype(jnp.int32)
        slots = owners * CAP + ranks
        placing = (
            (lax.broadcasted_iota(jnp.int32, (SLABS * CAP, ROWS), 0) == slots)
            .astype(jnp.float32)
            .astype(jnp.bfloat16)
        )
        rank_hits = (
            (lax.broadcasted_iota(jnp.int32, (128, ROWS), 0) % CAP == ranks)
            .astype(jnp.float32)
            .astype(jnp.bfloat16)
        )
        high = (labels // 32).astype(jnp.float32)
        low = (labels % 32 + 1).astype(jnp.float32)
        codes = jnp.concatenate([hits_f * high, hits_f * low], axis=0).astype(jnp.bfloat16)
        placed_codes = lax.dot_general(
            codes, rank_hits, (((1,), (1,)), ((), ())), preferred_element_type=jnp.float32
        )
        label_rows = placed_codes[:SLABS] * 32.0 + placed_codes[SLABS:] - 1.0
        for k in range(SLABS):
            sent_labels[core, k] = label_rows[k : k + 1, :]
        loads[2].wait()
        placed = jnp.dot(placing, values_ref[...], preferred_element_type=jnp.float32)
        sent[core] = placed.astype(jnp.bfloat16).reshape(SLABS, CAP, 128)

    def green_copy(block, piece, d, source=None):
        ref = green.at[block * 2 + piece // 2, piece % 2]
        to = {"slab": slab + 2 * d}
        return remote(source or ref, ref, green_send, green_recv.at[block, piece], to)

    def pair_copy(block, piece):
        ref = green.at[block * 2 + piece // 2, piece % 2]
        return remote(ref, ref, pair_send, pair_recv.at[block], partner)

    def green_wait(block, piece):
        arrived(green.at[block * 2 + piece // 2, piece % 2], green_recv.at[block, piece])

    def green_start(piece):
        source = green_hbm.at[piece] if piece < 2 else None

        @pl.when(z < CHIPS - 1)
        def _():
            green_copy(z, piece, 1, source).start()

        @pl.when(z > 0)
        def _():
            green_copy(z, piece, -1, source).start()

    def green_step(step):
        for piece in range(4):

            @pl.when(z >= step)
            def _():
                green_wait(z - step, piece)

                @pl.when(z < CHIPS - 1)
                def _():
                    green_copy(z - step, piece, 1).start()

                pair_copy(z - step, piece).start()

            @pl.when(z + step < CHIPS)
            def _():
                green_wait(z + step, piece)

                @pl.when(z > 0)
                def _():
                    green_copy(z + step, piece, -1).start()

                pair_copy(z + step, piece).start()

    def trace_send(chip):
        to = {"slab": chip * 2 + core}
        owners_of = pl.ds(chip * 2, 2)
        remote(sent.at[:, owners_of], got.at[z], trace_sem.at[0], trace_recv.at[z], to).start()
        remote(
            sent_labels.at[:, owners_of], got_labels.at[z], trace_sem.at[1], label_recv.at[z], to
        ).start()

    def all_traces(i):
        arrived((got, got_labels)[i].at[pl.ds(0, CHIPS - 1)], trace_sem.at[i])

    def assemble(chip, first):
        low_lanes = lax.broadcasted_iota(jnp.int32, (1, 128), 1) < CAP
        rows_f = lax.broadcasted_iota(jnp.int32, (ROWS, 128), 0).astype(jnp.float32)
        for owner in range(2):
            row = jnp.where(low_lanes, got_labels[chip, 0, owner], got_labels[chip, 1, owner])
            picks = (rows_f == row).astype(jnp.float32).astype(jnp.bfloat16)
            term = jnp.dot(
                picks, got[chip, :, owner].reshape(128, 128), preferred_element_type=jnp.float32
            )
            gathered[owner] = term if first else gathered[owner] + term

    def chip_of(n):
        m = jnp.minimum(z, CHIPS - 1 - z)
        side = z + jnp.where(n % 2 == 1, -((n + 1) // 2), n // 2)
        rest = jnp.where(z < CHIPS // 2, n, CHIPS - 1 - n)
        return jnp.where(n <= 2 * m, side, rest)

    def trace_steps(first, last):
        for s in range(first, last + 1):

            @pl.when(z >= s)
            def _():
                if s > 1:
                    pl.semaphore_wait(from_left.at[s - 2], 1)

                @pl.when(z < CHIPS - 1)
                def _():
                    pl.semaphore_signal(
                        from_left.at[s - 1], inc=1, device_id=along(1), device_id_type=MESH
                    )

                trace_send(z - s)

            @pl.when(z + s < CHIPS)
            def _():
                if s > 1:
                    pl.semaphore_wait(from_right.at[s - 2], 1)

                @pl.when(z > 0)
                def _():
                    pl.semaphore_signal(
                        from_right.at[s - 1], inc=1, device_id=along(-1), device_id_type=MESH
                    )

                trace_send(z + s)

    def other_line():
        pl.semaphore_wait(across, 1)

        @pl.when(gap < CHIPS - 1)
        def _():
            pl.semaphore_signal(across, inc=1, device_id=along(-inward), device_id_type=MESH)

    def block_of(half, a, b, hh):
        return at(a, b, hh) if half == 0 else at(b, a, hh)

    def res_copy(half, a, b, hh, chunk, quarter, way, sem):
        first = half * ROWS + chunk * PART + max(quarter, 0) * (PART // 2)
        count = PART if quarter < 0 else PART // 2
        ref = res.at[block_of(half, a, b, hh), pl.ds(first, count), :]
        to = {"src": block_of(half, way[0], way[1], h)}
        remote(ref, ref, res_send, res_recv.at[sem], to).start()

    def give(turn, a, b):
        ref = res.at[at(a, b, (h, 1 - h)[turn // 2]), pl.ds(turn % 2 * PART, PART), :]
        remote(ref, ref, give_send, give_recv.at[turn], partner).start()

    RIGHT, LEFT, UP, DOWN = (1, 0), (-1, 0), (0, 1), (0, -1)

    def res_round(step, turn):
        hh, chunk = (h, 1 - h)[turn // 2], turn % 2

        def sem(number):
            return turn * 5 + number - 1

        if step > 0:
            ref = (
                res.at[0],
                res.at[0, pl.ds(0, ROWS), :],
                res.at[pl.ds(0, 3)],
                res.at[0],
                res.at[pl.ds(0, 2)],
            )[step - 1]
            arrived(ref, res_recv.at[sem(step)])
        for half in range(2):
            if step == 0:
                res_copy(half, 0, 0, hh, chunk, -1, RIGHT, sem(1))
                res_copy(half, 0, 0, hh, chunk, -1, LEFT, sem(1))
            elif step == 1:
                res_copy(half, -1, 0, hh, chunk, 0, RIGHT, sem(2))
                res_copy(half, 1, 0, hh, chunk, 1, LEFT, sem(2))
            elif step == 3:
                for a in (0, -1, 1):
                    res_copy(half, a, -1, hh, chunk, 0, UP, sem(5))
                    res_copy(half, a, 1, hh, chunk, 1, DOWN, sem(5))
            elif step == 4:
                res_copy(half, 2, -1, hh, chunk, 0, UP, sem(5))
                res_copy(half, 2, 1, hh, chunk, 1, DOWN, sem(5))
        if step < 3:
            for half in range(2):
                number = sem(3 if step < 2 else 4)
                for a in ((0,), (-1, 1), (2,))[step]:
                    res_copy(half, a, 0, hh, chunk, -1, UP, number)
                    res_copy(half, a, 0, hh, chunk, -1, DOWN, number)
        for a, b in (
            ((0, 0),),
            ((-1, 0), (1, 0)),
            ((2, 0),),
            ((0, -1), (0, 1), (-1, -1), (-1, 1), (1, -1), (1, 1)),
            ((2, -1), (2, 1)),
            ((0, 2), (-1, 2), (1, 2), (2, 2)),
        )[step]:
            give(turn, a, b)

    @pl.when(core == 0)
    def _():
        pl.semaphore_wait(barrier, greeted)
        for piece in range(2):
            green_start(piece)

    @pl.when(core == 1)
    def _():
        pl.semaphore_wait(barrier, greeted)
        own_copy.start()

    place_traces()
    loads[3].wait()

    @pl.when(core == 0)
    def _():
        hand_labels.start()
        hand_values.start()
        arrived(own_block, own_sem.at[1])
        for piece in range(2, 4):
            green_start(piece)
        for piece in range(2):
            pair_copy(z, piece).start()
        for step in range(1, EARLY_STEPS + 1):
            if step == 2:

                @pl.when(gap == 0)
                def _():
                    pl.semaphore_wait(across, 1)
                    pl.semaphore_signal(
                        across, inc=1, device_id=along(inward, 1), device_id_type=MESH
                    )

            green_step(step)
        for turn in range(4):
            arrived(res.at[pl.ds(0, SRCS // 8)], give_recv.at[turn])

    @pl.when(core == 1)
    def _():
        arrived(sent_labels.at[0], hand_sem.at[3])
        arrived(sent.at[0], hand_sem.at[1])
        trace_steps(1, CHIPS - 1)
        for i in range(2):
            got[z, i] = sent[i, pl.ds(z * 2, 2)]
            got_labels[z, i] = sent_labels[i, pl.ds(z * 2, 2)]

        @pl.when(gap == 0)
        def _():
            pl.semaphore_signal(across, inc=1, device_id=partner, device_id_type=MESH)

        @pl.when(gap <= 4)
        def _():
            other_line()

        assemble(z, True)

        def next_chip(n, carry):
            chip = chip_of(n)
            arrived(got_labels.at[chip], label_recv.at[chip])
            arrived(got.at[chip], trace_recv.at[chip])
            assemble(chip, False)
            return carry

        lax.fori_loop(1, CHIPS, next_chip, 0)
        for owner in range(2):
            res[src, pl.ds(owner * ROWS, ROWS), :] = gathered[owner].astype(jnp.bfloat16)

        res_round(0, 0)
        res_round(0, 1)

        @pl.when(gap > 4)
        def _():
            other_line()

        twin = at(0, 0, 1 - h)
        for chunk in range(2):
            for half in range(2):
                ref = res.at[src, pl.ds(half * ROWS + chunk * PART, PART), :]
                remote(ref, ref, twin_send, twin_recv.at[chunk], {"src": twin}).start()
        for step, turn in ROUNDS:
            if step == 0:
                arrived(res.at[0, pl.ds(0, ROWS), :], twin_recv.at[turn - 2])
            res_round(step, turn)
        arrived(res.at[0], twin_send)

    acc_re[...] = jnp.zeros_like(acc_re)
    acc_im[...] = jnp.zeros_like(acc_im)
    loads[4].wait()

    def multiply(n, carry):
        block = chip_of(n)
        far = jnp.abs(block - z)
        before = jnp.abs(chip_of(jnp.maximum(n - 1, 0)) - z)

        @pl.when((core == 0) & (far > EARLY_STEPS) & (far > before))
        def _():
            green_step(far)

        @pl.when((core == 1) & (far == 0))
        def _():
            arrived(green.at[0], pair_recv.at[block])

        @pl.when((core == 1) & (far > 0))
        def _():
            arrived(green.at[pl.ds(0, 2)], pair_recv.at[block])

        rows = pl.ds(pl.multiple_of(core * ROWS, ROWS), ROWS)
        left = jnp.concatenate([res[4 * block + i, rows, :] for i in range(4)], axis=1)
        right_re, right_im = [], []
        for i in range(4):
            half = pl.ds(i % 2 * CAP, CAP)
            g_re, g_im = (green[block * 2 + i // 2, c, half, :] for c in range(2))
            right_re += [g_re, g_im]
            right_im += [g_im, -g_re]
        right_re, right_im = (jnp.concatenate(r, axis=0) for r in (right_re, right_im))
        acc_re[...] += jnp.dot(left, right_re, preferred_element_type=jnp.float32)
        acc_im[...] += jnp.dot(left, right_im, preferred_element_type=jnp.float32)
        return carry

    lax.fori_loop(0, CHIPS, multiply, 0)
    partial = jnp.sum(
        fields[0].astype(jnp.float32) * acc_re[...] - fields[1].astype(jnp.float32) * acc_im[...],
        axis=0,
        keepdims=True,
    )
    parts[slab] = partial
    for d in range(1, SLABS):
        to = {"slab": (slab + d) % SLABS}
        remote(parts.at[slab], parts.at[slab], sum_sem.at[0], sum_sem.at[1], to).start()

    end = (z == 0) | (z == CHIPS - 1)

    @pl.when(core == 0)
    def _():
        hand_values.wait_send()
        hand_labels.wait_send()
        arrived(green.at[pl.ds(0, SLABS - 1)], pair_send)

        @pl.when(end)
        def _():
            arrived(res.at[pl.ds(0, 2)], green_send)

        @pl.when(jnp.logical_not(end))
        def _():
            arrived(res.at[pl.ds(0, 2 * CHIPS + 2)], green_send)

    @pl.when(core == 1)
    def _():
        own_copy.wait_send()
        all_traces(0)
        all_traces(1)
        arrived(res.at[pl.ds(0, SRCS - 2)], res_send)
        arrived(res.at[pl.ds(0, SRCS // 2)], give_send)

    arrived(parts.at[pl.ds(0, SLABS - 1)], sum_sem.at[1])
    arrived(parts.at[pl.ds(0, SLABS - 1)], sum_sem.at[0])


def total(parts_ref, out_ref):
    out_ref[...] = jnp.sum(parts_ref[...], axis=0)


def on_device(trace_values, trace_owner, trace_source, source_fields, green_fields):
    dma = pltpu.SemaphoreType.DMA
    vmem = pl.BlockSpec(memory_space=pltpu.VMEM)
    parts = pl.pallas_call(
        kernel,
        out_shape=jax.ShapeDtypeStruct((SLABS, 1, CELLS), jnp.float32),
        in_specs=[pl.BlockSpec(memory_space=pltpu.HBM)] * 5,
        out_specs=vmem,
        scratch_shapes=[
            pltpu.VMEM((1, ROWS), jnp.int32),
            pltpu.VMEM((1, ROWS), jnp.int32),
            pltpu.VMEM((ROWS, 128), jnp.bfloat16),
            pltpu.VMEM((2, SLABS, CAP, 128), jnp.bfloat16),
            pltpu.VMEM((2, SLABS, 1, 128), jnp.float32),
            pltpu.VMEM((CHIPS, 2, 2, CAP, 128), jnp.bfloat16),
            pltpu.VMEM((CHIPS, 2, 2, 1, 128), jnp.float32),
            pltpu.VMEM((2, ROWS, 128), jnp.float32),
            pltpu.VMEM((SRCS, 2 * ROWS, 128), jnp.bfloat16),
            pltpu.VMEM((SLABS, 2, 128, CELLS), jnp.bfloat16),
            pltpu.VMEM((2, ROWS, CELLS), jnp.bfloat16),
            pltpu.VMEM((ROWS, CELLS), jnp.float32),
            pltpu.VMEM((ROWS, CELLS), jnp.float32),
            dma((5,)),
            dma((4,)),
            dma((2,)),
            dma((CHIPS,)),
            dma((CHIPS,)),
            dma,
            dma((CHIPS, 4)),
            dma,
            dma((CHIPS,)),
            dma((2,)),
            dma,
            dma((2,)),
            dma,
            dma((20,)),
            dma,
            dma((4,)),
            dma((2,)),
            pltpu.SemaphoreType.REGULAR((CHIPS - 1,)),
            pltpu.SemaphoreType.REGULAR((CHIPS - 1,)),
            pltpu.SemaphoreType.REGULAR,
        ],
        compiler_params=pltpu.CompilerParams(
            collective_id=0, has_side_effects=True, vmem_limit_bytes=60 * 1024 * 1024
        ),
    )(
        trace_owner.reshape(1, ROWS),
        trace_source.reshape(1, ROWS),
        trace_values[0],
        source_fields,
        green_fields,
    )
    out = pl.pallas_call(
        total,
        out_shape=jax.ShapeDtypeStruct((1, CELLS), jnp.float32),
        in_specs=[vmem],
        out_specs=vmem,
    )(parts)
    return out.reshape(CELLS)


def solution(mesh):
    in_specs = (
        P("src", "slab", None),
        P("src", "slab", None),
        P("src", "slab"),
        P(None, "slab", "src"),
        P(None, "slab", "src"),
    )
    return jax.shard_map(
        on_device, mesh=mesh, in_specs=in_specs, out_specs=P("src"), check_vma=False
    )
```
